256 devices in a mesh: outer: 32 (over z_lo, x, core), inner: 8 (over y, z_hi).
Axes of the slice: x: 4, y: 4, z: 8 (z_hi: 2, z_lo: 4; z = z_hi * 4 + z_lo), core: 2. Of those that a mesh axis runs over, the one named last changes fastest.
Arguments:
- qkv: bfloat16 [16384, 8, 10, 128], P(('outer', 'inner')), may hold values from -96 to 96
- key_codes: int32 [4096, 8, 16], P('outer', 'inner'), may hold values from 0 to 255
- codebooks: bfloat16 [8, 256, 128], P('inner'), may hold values from -4 to 4
- value_codes: bfloat16 [4096, 8, 128], P('outer', 'inner'), may hold values from -4 to 4
- value_scales: float32 [4096, 8], P('outer', 'inner'), may hold values from 0.25 to 4
- block_ids: int32 [32], P('outer'), may hold values from 0 to 31, each once
Outputs:
- attended: bfloat16 [16384, 8, 8, 128], P(('outer', 'inner'))
The draws below stay inside these ranges and needn't reach their ends.
All inputs are finite; a program needn't handle non-finite values.
Results may differ from the reference program's by a relative error of at most 0.011.
Values may be sent and summed in bfloat16 or wider, within the bound.
A program may use at most 64 MiB of HBM per device.

```python
import math
import jax
import jax.numpy as jnp
from jax import lax

KV = 8
HEAD = 128
CODES = 256
BLOCK = 128
GQ = 8
GROUPS = 16
STRETCH = 512
TOKENS = 16384
PREFIX = 4096
N_OUTER = 32


def draw_qkv(key, part):
    key_query, key_key, key_value = jax.random.split(jax.random.fold_in(key, 7), 3)
    query_shape = (TOKENS, KV, GQ, HEAD)
    single_shape = (TOKENS, KV, 1, HEAD)
    queries = 2.5 * jax.random.truncated_normal(key_query, -4.0, 4.0, query_shape, jnp.float32)
    keys_new = jax.random.truncated_normal(key_key, -4.0, 4.0, single_shape, jnp.float32)
    values_new = jax.random.truncated_normal(key_value, -4.0, 4.0, single_shape, jnp.float32)
    return jnp.concatenate([queries, keys_new, values_new], axis=2).astype(jnp.bfloat16)


def touch_ends(result, rng, least, top_value):
    longest = result.shape.index(max(result.shape))
    spots = []
    for shift in (0, 1):
        where = [jax.random.randint(jax.random.fold_in(rng, axis), (), 0, length) for axis, length in enumerate(result.shape)]
        where[longest] = (where[longest] + shift) % result.shape[longest]
        spots.append(tuple(where))
    return result.at[spots[0]].set(least).at[spots[1]].set(top_value)


def level_of(key, shape, cuts, low, largest):
    gain = 1.0
    for dim, shards_of in cuts:
        draws = jax.random.uniform(jax.random.fold_in(jax.random.fold_in(key, 6), dim), (shards_of,), jnp.float32, low / len(cuts), largest / len(cuts))
        gain = gain * jnp.repeat(jnp.exp(draws), shape[dim] // shards_of).reshape((-1,) + (1,) * (len(shape) - 1 - dim))
    return gain


def bell_draw(key, shape, spread, bound, cuts=(), kind=jnp.bfloat16):
    array = jax.random.normal(key, shape, jnp.float32) * spread
    if len(cuts) > 0:
        array = level_of(key, shape, cuts, -0.22, 0.18) * array
    return jnp.clip(array, min=-bound, max=bound).astype(kind)


def setup_inputs(seed: int = 0) -> dict:
    streams_of = jax.random.split(jax.random.key(seed), 7)
    qkv = draw_qkv(jax.random.fold_in(streams_of[6], 71), 0)
    key_codes = touch_ends(jax.random.randint(streams_of[1], (PREFIX, KV, GROUPS), 0, CODES), jax.random.fold_in(streams_of[1], 1), 0, CODES - 1).astype(jnp.int32)
    codebooks = bell_draw(streams_of[2], (KV, CODES, HEAD), 1.0, 4.0, ((0, 8),))
    value_codes = bell_draw(streams_of[3], (PREFIX, KV, HEAD), 1.0, 4.0, ((0, 32), (1, 8)))
    value_scales = jnp.clip(jnp.exp(math.log(4.0) - 2.7725887 * jax.random.uniform(streams_of[4], (PREFIX, KV), jnp.float32) ** level_of(streams_of[4], (PREFIX, KV), ((0, 32), (1, 8)), -0.2, 0.2)), 0.25, 4.0)
    block_ids = jax.random.permutation(streams_of[5], N_OUTER).astype(jnp.int32)
    return dict(qkv=qkv, key_codes=key_codes, codebooks=codebooks, value_codes=value_codes, value_scales=value_scales, block_ids=block_ids)


rope_base = 500000.0


def rotate(tensor, position):
    half_dim = tensor.shape[-1] // 2
    ladder = jnp.arange(half_dim, dtype=jnp.float32)
    inverse = jnp.exp(ladder * jnp.float32(-2.0 * math.log(rope_base) / tensor.shape[-1]))
    angles = position.astype(jnp.float32)[:, None] * inverse[None, :]
    target = (position.shape[0],) + (1,) * (tensor.ndim - 2) + (half_dim,)
    cosine = jnp.cos(angles).reshape(target)
    sine_part = jnp.sin(angles).reshape(target)
    floats = tensor.astype(jnp.float32)
    first_half = floats[..., :half_dim]
    second_half = floats[..., half_dim:]
    return jnp.concatenate([first_half * cosine - second_half * sine_part, second_half * cosine + first_half * sine_part], axis=-1)


def reference(qkv, key_codes, codebooks, value_codes, value_scales, block_ids):
    code_table = codebooks.reshape(KV, CODES, GROUPS, 8)
    picked = code_table[jnp.arange(KV, dtype=jnp.int32)[None, :, None], key_codes, jnp.arange(GROUPS, dtype=jnp.int32)[None, None, :]]
    raw_keys = picked.reshape(PREFIX, KV, HEAD)
    prefix_rows = jnp.arange(PREFIX, dtype=jnp.int32)
    prefix_pos = block_ids[prefix_rows // BLOCK] * BLOCK + prefix_rows % BLOCK
    prefix_keys = rotate(raw_keys, prefix_pos).astype(jnp.bfloat16)
    prefix_values = (value_codes.astype(jnp.float32) * value_scales[:, :, None]).astype(jnp.bfloat16)
    tokens = jnp.arange(TOKENS, dtype=jnp.int32)
    stretch_pos = PREFIX + tokens % STRETCH
    queries = rotate(qkv[:, :, :GQ, :], stretch_pos).astype(jnp.bfloat16)
    stretch_keys = rotate(qkv[:, :, GQ, :], stretch_pos).astype(jnp.bfloat16)
    stretch_values = qkv[:, :, GQ + 1, :]
    local_pos = jnp.arange(STRETCH, dtype=jnp.int32)
    allowed = jnp.concatenate([jnp.ones((STRETCH, PREFIX), dtype=bool), local_pos[None, :] <= local_pos[:, None]], axis=1)
    score_scale = HEAD ** -0.5

    def attend_group(pair_index):
        stretch_index = pair_index // KV
        kv_index = pair_index % KV
        first_row = (stretch_index * STRETCH).astype(jnp.int32)
        query_rows = lax.dynamic_index_in_dim(lax.dynamic_slice_in_dim(queries, first_row, STRETCH, 0), kv_index, 1, False)
        own_keys = lax.dynamic_index_in_dim(lax.dynamic_slice_in_dim(stretch_keys, first_row, STRETCH, 0), kv_index, 1, False)
        own_values = lax.dynamic_index_in_dim(lax.dynamic_slice_in_dim(stretch_values, first_row, STRETCH, 0), kv_index, 1, False)
        key_rows = jnp.concatenate([lax.dynamic_index_in_dim(prefix_keys, kv_index, 1, False), own_keys], axis=0)
        value_rows = jnp.concatenate([lax.dynamic_index_in_dim(prefix_values, kv_index, 1, False), own_values], axis=0)
        scores = jnp.einsum("tqd,nd->tqn", query_rows.astype(jnp.float32), key_rows.astype(jnp.float32)) * score_scale
        scores = jnp.where(allowed[:, None, :], scores, -jnp.inf)
        row_max = jnp.max(scores, axis=-1, keepdims=True)
        weights = jnp.exp(scores - row_max)
        weight_sum = jnp.sum(weights, axis=-1, keepdims=True)
        rounded = lax.optimization_barrier(weights.astype(jnp.bfloat16))
        mixed_rows = jnp.einsum("tqn,nd->tqd", rounded.astype(jnp.float32), value_rows.astype(jnp.float32))
        return (mixed_rows / weight_sum).astype(jnp.bfloat16)

    stacked = lax.map(attend_group, jnp.arange(N_OUTER * KV, dtype=jnp.int32))
    stacked = stacked.reshape(N_OUTER, KV, STRETCH, GQ, HEAD).transpose(0, 2, 1, 3, 4)
    return stacked.reshape(TOKENS, KV, GQ, HEAD)
```

```python
import functools
import math

import jax
import jax.numpy as jnp
from jax import lax
from jax.experimental import pallas as pl
from jax.experimental.pallas import tpu as pltpu
from jax.sharding import PartitionSpec as P

rope_base = 500000.0
NX, NY, NZ, NH = 4, 4, 8, 4
BLOCK, HEAD, GQ, LOCAL = 128, 128, 8, 64
ROWS = 256
SCALE = 128**-0.5 * math.log2(math.e)
NT = (((1,), (1,)), ((), ()))


def rotate(tensor, position):
    half_dim = tensor.shape[-1] // 2
    ladder = jnp.arange(half_dim, dtype=jnp.float32)
    inverse = jnp.exp(ladder * jnp.float32(-2.0 * math.log(rope_base) / tensor.shape[-1]))
    angles = position.astype(jnp.float32)[:, None] * inverse[None, :]
    target = (position.shape[0],) + (1,) * (tensor.ndim - 2) + (half_dim,)
    cosine = jnp.cos(angles).reshape(target)
    sine_part = jnp.sin(angles).reshape(target)
    floats = tensor.astype(jnp.float32)
    first_half = floats[..., :half_dim]
    second_half = floats[..., half_dim:]
    return jnp.concatenate(
        [
            first_half * cosine - second_half * sine_part,
            second_half * cosine + first_half * sine_part,
        ],
        axis=-1,
    )


def decode_block(key_codes, codebooks):
    block_rows, kv_local, group_count = key_codes.shape
    entries = codebooks.shape[1]
    head_dim = codebooks.shape[2]
    ladder = lax.broadcasted_iota(jnp.int32, (1, 1, 1, entries), 3).astype(jnp.float32)
    one_hot = (key_codes.astype(jnp.float32)[..., None] == ladder).astype(jnp.bfloat16)
    code_table = codebooks.reshape(kv_local, entries, group_count, head_dim // group_count)
    decoded = jnp.einsum("bkgc,kcgd->bkgd", one_hot, code_table, preferred_element_type=jnp.float32)
    return decoded.reshape(block_rows, kv_local, head_dim)


def kernel(q_in, sk_in, sv_in, kv_in, out, kv, qb, sk, sv, rk, rv, ob, sa, sb, ma, mb,
           send, rs, rq, rsk, rsv, rrk, rrv, rx, ro, loc, osend):
    o = lax.axis_index("outer")
    i = lax.axis_index("inner")
    zl, x, c = o // 8, (o // 2) % NX, o % 2
    y, zh = i // 2, i % 2
    z = zh * NH + zl

    def dev(dx=0, dy=0, dz=0, dc=0):
        x1, y1, z1, c1 = (x + dx) % NX, (y + dy) % NY, (z + dz) % NZ, (c + dc) % 2
        return {"outer": (z1 % NH) * 8 + x1 * 2 + c1, "inner": y1 * 2 + z1 // NH}

    def slot(dz, dx, dc=0):
        return (((z + dz) % NZ) * NX + (x + dx) % NX) * 2 + (c + dc) % 2

    peers = [dev(dz=1), dev(dz=-1), dev(dx=1), dev(dx=-1), dev(dc=1)]
    peers += [dev(dy=d) for d in (1, 2, 3)]
    peers += [dev(dy=d, dz=s) for d in range(4) for s in (2, -2)]
    barrier = pltpu.get_barrier_semaphore()
    for peer in peers:
        pl.semaphore_signal(barrier, inc=1, device_id=peer, device_id_type=pl.DeviceIdType.MESH)
    pl.semaphore_wait(barrier, len(peers))

    sent = []

    def put(src, dst, recv_sem, to):
        copy = pltpu.make_async_remote_copy(
            src_ref=src, dst_ref=dst, send_sem=send.at[len(sent)], recv_sem=recv_sem,
            device_id=to, device_id_type=pl.DeviceIdType.MESH)
        copy.start()
        sent.append(copy)

    def got(dst, recv_sem):
        pltpu.make_async_copy(dst, dst, recv_sem).wait()

    kept = []

    def keep(src, dst):
        copy = pltpu.make_async_copy(src, dst, loc.at[len(kept)])
        copy.start()
        kept.append(copy)

    own = slot(0, 0)
    for to in (dev(dz=1), dev(dz=-1), dev(dx=1), dev(dx=-1), dev(dc=1)):
        put(kv_in, kv.at[own], rs.at[own, 0], to)
    keep(kv_in, kv.at[own])
    for d in range(4):
        yd = (y + d) % NY
        pair = pl.ds(2 * yd, 2)
        put(sk_in.at[pair], rk.at[y], rrk.at[y], dev(dy=d, dz=2))
        put(sv_in.at[pair], rv.at[y], rrv.at[y], dev(dy=d, dz=-2))
        if d == 0:
            keep(sk_in.at[pair], sk.at[zh, y])
            keep(sv_in.at[pair], sv.at[zh, y])
        else:
            put(sk_in.at[pair], sk.at[zh, y], rsk.at[y], dev(dy=d))
            put(sv_in.at[pair], sv.at[zh, y], rsv.at[y], dev(dy=d))
    for hh in (zh, 1 - zh):
        for d in range(4):
            yd = (y + d) % NY
            if d == 0:
                keep(q_in.at[2 * yd + hh], qb.at[hh, y])
            else:
                put(q_in.at[2 * yd + hh], qb.at[hh, y], rq.at[hh, y], dev(dy=d))

    def spread(s):
        put(kv.at[s], kv.at[s], rs.at[s, 0], dev(dx=1))
        put(kv.at[s], kv.at[s], rs.at[s, 0], dev(dx=-1))
        put(kv.at[s], kv.at[s], rs.at[s, 0], dev(dc=1))

    for d in (1, 2, 3):
        for sign in (-1, 1):
            s = slot(sign * d, 0)
            got(kv.at[s], rs.at[s, 0])
            if d < 3:
                put(kv.at[s], kv.at[s], rs.at[s, 0], dev(dz=-sign))
            else:
                half = 0 if sign < 0 else 1
                put(kv.at[s, half], kv.at[s, half], rs.at[s, half], dev(dz=-sign))
            spread(s)
    s = slot(4, 0)
    got(kv.at[s, 0], rs.at[s, 0])
    got(kv.at[s, 1], rs.at[s, 1])
    spread(s)

    for src in range(NY):
        got(rk.at[src], rrk.at[src])
        got(rv.at[src], rrv.at[src])
    put(rk, sk.at[((z + 6) % NZ) // NH], rx.at[0], dev(dz=2))
    put(rv, sv.at[((z + 2) % NZ) // NH], rx.at[1], dev(dz=-2))

    order = (0, -1, 1, -2, 2, -3, 3, 4)
    for dz in order:
        for sign in (-1, 1):
            s = slot(dz, sign)
            got(kv.at[s], rs.at[s, 0])
            half = 0 if sign < 0 else 1
            put(kv.at[s, half], kv.at[s, half], rs.at[s, half], dev(dx=-sign))
            put(kv.at[s], kv.at[s], rs.at[s, 0], dev(dc=1))
    for dz in order:
        s = slot(dz, 2)
        got(kv.at[s, 0], rs.at[s, 0])
        got(kv.at[s, 1], rs.at[s, 1])
        put(kv.at[s], kv.at[s], rs.at[s, 0], dev(dc=1))
    for dz in order:
        for dx in range(4):
            s = slot(dz, dx, 1)
            got(kv.at[s], rs.at[s, 0])
    for d in (1, 2, 3):
        src = (y + d) % NY
        got(sk.at[zh, src], rsk.at[src])
        got(sv.at[zh, src], rsv.at[src])
        for hh in range(2):
            got(qb.at[hh, src], rq.at[hh, src])
    got(sk.at[1 - zh], rx.at[0])
    got(sv.at[1 - zh], rx.at[1])
    for copy in kept:
        copy.wait()

    def unit(u):
        return (zh + u // 4) % 2, (y + 1 + u % 4) % NY

    def keys_of(hh, n):
        if n < 8:
            part = kv[pl.ds(hh * 32 + 4 * n, 4), 0]
            return part.reshape(4 * BLOCK, HEAD)
        return sk[n - 8, :, hh].reshape(4 * LOCAL, HEAD)

    def values_of(hh, n):
        if n < 8:
            part = kv[pl.ds(hh * 32 + 4 * n, 4), 1]
            return part.reshape(4 * BLOCK, HEAD)
        return sv[n - 8, :, hh].reshape(4 * LOCAL, HEAD)

    spans = [(512 * n, 512) for n in range(8)] + [(4096, 256), (4352, 256)]

    def query_tile(t):
        hh, src = unit(t // 2)
        floats = qb[hh, src, pl.ds(pl.multiple_of((t % 2) * ROWS, ROWS), ROWS), :].astype(jnp.float32) * SCALE
        high = floats.astype(jnp.bfloat16)
        low = (floats - high.astype(jnp.float32)).astype(jnp.bfloat16)
        return jnp.concatenate([high, low], axis=1)

    def score(t, n, buf):
        hh, src = unit(t // 2)
        keys = keys_of(hh, n)
        first, size = spans[n]
        keys = jnp.concatenate([keys, keys], axis=1)
        s = lax.dot_general(query_tile(t), keys, NT, preferred_element_type=jnp.float32)
        if n >= 8:
            token = (2 * src + zh) * LOCAL + (t % 2) * (ROWS // GQ)
            row = token + lax.broadcasted_iota(jnp.int32, (ROWS, size), 0) // GQ
            col = lax.broadcasted_iota(jnp.int32, (ROWS, size), 1)
            col = (col // LOCAL) * (2 * LOCAL) + (n - 8) * LOCAL + col % LOCAL
            s = jnp.where(col <= row, s, -1e30)
        buf[:, first:first + size] = s
        top = s[:, :128]
        for j in range(1, size // 128):
            top = jnp.maximum(top, s[:, j * 128:(j + 1) * 128])
        return top

    def weigh(t, n, buf, top):
        hh, _ = unit(t // 2)
        first, size = spans[n]
        weights = jnp.exp2(buf[:, first:first + size] - top).astype(jnp.bfloat16)
        values = values_of(hh, n)
        values = jnp.concatenate([values, jnp.ones_like(values)], axis=1)
        return jnp.dot(weights, values, preferred_element_type=jnp.float32)

    def stage(tn, bufn, mn, tc, bufc, mc):
        top, total = None, None
        for n in range(len(spans)):
            if tn is not None:
                part = score(tn, n, bufn)
                top = part if top is None else jnp.maximum(top, part)
            if tc is not None:
                part = weigh(tc, n, bufc, mc[:, :1])
                total = part if total is None else total + part
        if tn is not None:
            mn[...] = jnp.broadcast_to(jnp.max(top, axis=1, keepdims=True), mn.shape)
        if tc is not None:
            hh, src = unit(tc // 2)
            result = (total[:, :HEAD] / total[:, HEAD:]).reshape(ROWS // GQ, GQ, HEAD)
            at = pl.ds(pl.multiple_of((tc % 2) * (ROWS // GQ), ROWS // GQ), ROWS // GQ)
            ob[hh, src, at] = result.astype(jnp.bfloat16)

    def result_copy(u):
        hh, src = unit(u)
        return pltpu.make_async_remote_copy(
            src_ref=ob.at[hh, src], dst_ref=out.at[:, 2 * y + hh],
            send_sem=osend.at[u], recv_sem=ro.at[hh, y],
            device_id={"outer": o, "inner": src * 2 + zh}, device_id_type=pl.DeviceIdType.MESH)

    def own_copy(u):
        hh, src = unit(u)
        return pltpu.make_async_copy(ob.at[hh, src], out.at[:, 2 * y + hh], osend.at[u])

    stage(0, sa, ma, None, None, None)

    def body(u, carry):
        stage(2 * u + 1, sb, mb, 2 * u, sa, ma)
        stage(jnp.minimum(2 * u + 2, 15), sa, ma, 2 * u + 1, sb, mb)

        @pl.when(u % 4 < 3)
        def _():
            result_copy(u).start()

        @pl.when(u % 4 == 3)
        def _():
            own_copy(u).start()

        return carry

    lax.fori_loop(0, 8, body, 0)

    for copy in sent:
        copy.wait_send()
    for u in range(8):
        if u % 4 == 3:
            own_copy(u).wait()
        else:
            result_copy(u).wait_send()
    for hh in range(2):
        for d in (1, 2, 3):
            src = (y + d) % NY
            got(out.at[:, 2 * src + hh], ro.at[hh, src])


def shards(qkv, key_codes, codebooks, value_codes, value_scales, block_ids):
    block_rows = key_codes.shape[0]
    prefix_len = block_rows * lax.axis_size("outer")
    prefix_values = (value_codes.astype(jnp.float32) * value_scales[:, :, None]).astype(jnp.bfloat16)
    own_pos = block_ids[0] * block_rows + jnp.arange(block_rows, dtype=jnp.int32)
    prefix_keys = rotate(decode_block(key_codes, codebooks), own_pos).astype(jnp.bfloat16)
    kv_in = jnp.stack([prefix_keys[:, 0], prefix_values[:, 0]])
    stretch_pos = prefix_len + lax.axis_index("inner") * LOCAL + jnp.arange(LOCAL, dtype=jnp.int32)
    rotated = rotate(qkv[:, :, :GQ + 1], stretch_pos).astype(jnp.bfloat16)
    q_in = rotated[:, :, :GQ].transpose(1, 0, 2, 3).reshape(8, LOCAL * GQ, HEAD)
    sk_in = rotated[:, :, GQ].transpose(1, 0, 2)
    sv_in = qkv[:, :, GQ + 1].transpose(1, 0, 2)

    bf, f32 = jnp.bfloat16, jnp.float32
    dma = pltpu.SemaphoreType.DMA
    return pl.pallas_call(
        kernel,
        out_shape=jax.ShapeDtypeStruct((LOCAL, 8, GQ, HEAD), bf),
        in_specs=[pl.BlockSpec(memory_space=pltpu.VMEM)] * 4,
        out_specs=pl.BlockSpec(memory_space=pl.ANY),
        scratch_shapes=[
            pltpu.VMEM((64, 2, BLOCK, HEAD), bf),
            pltpu.VMEM((2, 4, LOCAL * GQ, HEAD), bf),
            pltpu.VMEM((2, 4, 2, LOCAL, HEAD), bf),
            pltpu.VMEM((2, 4, 2, LOCAL, HEAD), bf),
            pltpu.VMEM((4, 2, LOCAL, HEAD), bf),
            pltpu.VMEM((4, 2, LOCAL, HEAD), bf),
            pltpu.VMEM((2, 4, LOCAL, GQ, HEAD), bf),
            pltpu.VMEM((ROWS, 4608), f32),
            pltpu.VMEM((ROWS, 4608), f32),
            pltpu.VMEM((ROWS, 128), f32),
            pltpu.VMEM((ROWS, 128), f32),
            dma((128,)), dma((64, 2)), dma((2, 4)), dma((4,)), dma((4,)), dma((4,)), dma((4,)),
            dma((2,)), dma((2, 4)), dma((8,)), dma((8,)),
        ],
        compiler_params=pltpu.CompilerParams(
            collective_id=0, has_side_effects=True, vmem_limit_bytes=60 * 2**20),
    )(q_in, sk_in, sv_in, kv_in)


def solution(mesh):
    return jax.shard_map(
        shards,
        mesh=mesh,
        in_specs=(
            P(("outer", "inner"), None, None, None),
            P("outer", "inner", None),
            P("inner", None, None),
            P("outer", "inner", None),
            P("outer", "inner"),
            P("outer"),
        ),
        out_specs=P(("outer", "inner"), None, None, None),
        check_vma=False,
    )
```

```python
import functools
import math

import jax
import jax.numpy as jnp
from jax import lax
from jax.experimental import pallas as pl
from jax.experimental.pallas import tpu as pltpu
from jax.sharding import PartitionSpec as P

rope_base = 500000.0
NX, NY, NZ, NH = 4, 4, 8, 4
BLOCK, HEAD, GQ, LOCAL = 128, 128, 8, 64
ROWS = 256
SCALE = 128**-0.5 * math.log2(math.e)
NT = (((1,), (1,)), ((), ()))


def rotate(tensor, position):
    half_dim = tensor.shape[-1] // 2
    ladder = jnp.arange(half_dim, dtype=jnp.float32)
    inverse = jnp.exp(ladder * jnp.float32(-2.0 * math.log(rope_base) / tensor.shape[-1]))
    angles = position.astype(jnp.float32)[:, None] * inverse[None, :]
    target = (position.shape[0],) + (1,) * (tensor.ndim - 2) + (half_dim,)
    cosine = jnp.cos(angles).reshape(target)
    sine_part = jnp.sin(angles).reshape(target)
    floats = tensor.astype(jnp.float32)
    first_half = floats[..., :half_dim]
    second_half = floats[..., half_dim:]
    return jnp.concatenate(
        [
            first_half * cosine - second_half * sine_part,
            second_half * cosine + first_half * sine_part,
        ],
        axis=-1,
    )


def decode_block(key_codes, codebooks):
    block_rows, kv_local, group_count = key_codes.shape
    entries = codebooks.shape[1]
    head_dim = codebooks.shape[2]
    ladder = lax.broadcasted_iota(jnp.int32, (1, 1, 1, entries), 3).astype(jnp.float32)
    one_hot = (key_codes.astype(jnp.float32)[..., None] == ladder).astype(jnp.bfloat16)
    code_table = codebooks.reshape(kv_local, entries, group_count, head_dim // group_count)
    decoded = jnp.einsum("bkgc,kcgd->bkgd", one_hot, code_table, preferred_element_type=jnp.float32)
    return decoded.reshape(block_rows, kv_local, head_dim)


def kernel(q_in, sk_in, sv_in, kv_in, out, kv, qb, sk, sv, rk, rv, ob, sa, sb, ma, mb,
           send, rs, rq, rsk, rsv, rrk, rrv, rx, ro, loc, osend):
    o = lax.axis_index("outer")
    i = lax.axis_index("inner")
    zl, x, c = o // 8, (o // 2) % NX, o % 2
    y, zh = i // 2, i % 2
    z = zh * NH + zl

    def dev(dx=0, dy=0, dz=0, dc=0):
        x1, y1, z1, c1 = (x + dx) % NX, (y + dy) % NY, (z + dz) % NZ, (c + dc) % 2
        return {"outer": (z1 % NH) * 8 + x1 * 2 + c1, "inner": y1 * 2 + z1 // NH}

    def slot(dz, dx, dc=0):
        return (((z + dz) % NZ) * NX + (x + dx) % NX) * 2 + (c + dc) % 2

    peers = [dev(dz=1), dev(dz=-1), dev(dx=1), dev(dx=-1), dev(dc=1)]
    peers += [dev(dy=d) for d in (1, 2, 3)]
    peers += [dev(dy=d, dz=s) for d in range(4) for s in (2, -2)]
    barrier = pltpu.get_barrier_semaphore()
    for peer in peers:
        pl.semaphore_signal(barrier, inc=1, device_id=peer, device_id_type=pl.DeviceIdType.MESH)
    pl.semaphore_wait(barrier, len(peers))

    sent, ends = [], []
    likes = {r.shape: r for r in (kv.at[0], kv.at[0, 0], rk.at[0], rk, qb.at[0, 0])}

    def put(src, dst, recv_sem, to):
        copy = pltpu.make_async_remote_copy(
            src_ref=src, dst_ref=dst, send_sem=send.at[len(sent)], recv_sem=recv_sem,
            device_id=to, device_id_type=pl.DeviceIdType.MESH)
        copy.start()
        index = len(sent)
        sent.append(index)
        like = likes[src.shape]
        ends.append(lambda: pltpu.make_async_copy(like, like, send.at[index]).wait())

    def got(dst, recv_sem):
        pltpu.make_async_copy(dst, dst, recv_sem).wait()

    kept = []

    def keep(src, dst):
        copy = pltpu.make_async_copy(src, dst, loc.at[len(kept)])
        copy.start()
        kept.append(copy)

    own = slot(0, 0)
    for to in (dev(dz=1), dev(dz=-1), dev(dx=1), dev(dx=-1), dev(dc=1)):
        put(kv_in, kv.at[own], rs.at[own, 0], to)
    keep(kv_in, kv.at[own])
    for d in range(4):
        yd = (y + d) % NY
        pair = pl.ds(2 * yd, 2)
        put(sk_in.at[pair], rk.at[y], rrk.at[y], dev(dy=d, dz=2))
        put(sv_in.at[pair], rv.at[y], rrv.at[y], dev(dy=d, dz=-2))
        if d == 0:
            keep(sk_in.at[pair], sk.at[zh, y])
            keep(sv_in.at[pair], sv.at[zh, y])
        else:
            put(sk_in.at[pair], sk.at[zh, y], rsk.at[y], dev(dy=d))
            put(sv_in.at[pair], sv.at[zh, y], rsv.at[y], dev(dy=d))
    for hh in (zh, 1 - zh):
        for d in (0, 3, 1, 2):
            yd = (y + d) % NY
            if d == 0:
                keep(q_in.at[2 * yd + hh], qb.at[hh, y])
            else:
                put(q_in.at[2 * yd + hh], qb.at[hh, y], rq.at[hh, y], dev(dy=d))

    def spread(s):
        put(kv.at[s], kv.at[s], rs.at[s, 0], dev(dx=1))
        put(kv.at[s], kv.at[s], rs.at[s, 0], dev(dx=-1))
        put(kv.at[s], kv.at[s], rs.at[s, 0], dev(dc=1))

    def relay(dz):
        for sign in (-1, 1):
            s = slot(dz, sign)
            got(kv.at[s], rs.at[s, 0])
            half = 0 if sign < 0 else 1
            put(kv.at[s, half], kv.at[s, half], rs.at[s, half], dev(dx=-sign))
            put(kv.at[s], kv.at[s], rs.at[s, 0], dev(dc=1))

    def close(dz):
        s = slot(dz, 2)
        got(kv.at[s, 0], rs.at[s, 0])
        got(kv.at[s, 1], rs.at[s, 1])
        put(kv.at[s], kv.at[s], rs.at[s, 0], dev(dc=1))

    def ring(d):
        for sign in (-1, 1):
            s = slot(sign * d, 0)
            got(kv.at[s], rs.at[s, 0])
            if d < 3:
                put(kv.at[s], kv.at[s], rs.at[s, 0], dev(dz=-sign))
            else:
                half = 0 if sign < 0 else 1
                put(kv.at[s, half], kv.at[s, half], rs.at[s, half], dev(dz=-sign))

    first, last = (zl == 0).astype(jnp.int32), (zl == 3).astype(jnp.int32)
    third = (zl == 2).astype(jnp.int32)
    near = [0, 1 - 2 * last, 1 + first - 3 * last, 2 + first - 4 * third - 5 * last]
    near[1] = 1 - 2 * last
    near[2] = first * 2 + last * -2 + (1 - first - last) * -1
    near[3] = first * 3 + last * -3 + third * -2 + (1 - first - last - third) * 2

    def far(k):
        return (zh * 4 + 4 + k) - z

    ring(1)
    spread(slot(near[1], 0))
    relay(0)
    ring(2)
    spread(slot(near[2], 0))
    ring(3)
    spread(slot(near[3], 0))
    relay(near[1])
    for src in range(NY):
        got(rk.at[src], rrk.at[src])
        got(rv.at[src], rrv.at[src])
    put(rk, sk.at[((z + 6) % NZ) // NH], rx.at[0], dev(dz=2))
    put(rv, sv.at[((z + 2) % NZ) // NH], rx.at[1], dev(dz=-2))
    relay(near[2])
    relay(near[3])
    s = slot(4, 0)
    got(kv.at[s, 0], rs.at[s, 0])
    got(kv.at[s, 1], rs.at[s, 1])
    for k in range(4):
        spread(slot(far(k), 0))
    for k in range(4):
        close(near[k])
    for copy in kept:
        copy.wait()
    for k in range(4):
        for dx in range(4):
            s = slot(near[k], dx, 1)
            got(kv.at[s], rs.at[s, 0])

    def stretch_ready():
        for d in (1, 2, 3):
            src = (y + d) % NY
            got(sk.at[zh, src], rsk.at[src])
            got(sv.at[zh, src], rsv.at[src])
        got(sk.at[1 - zh], rx.at[0])
        got(sv.at[1 - zh], rx.at[1])

    def unit(u):
        k = min(u, 7 - u) if isinstance(u, int) else jnp.minimum(u, 7 - u)
        return (zh + u // 4) % 2, (y + k * (k + 1) // 2) % NY

    def keys_of(hh, n):
        if n < 8:
            part = kv[pl.ds(hh * 32 + 4 * n, 4), 0]
            return part.reshape(4 * BLOCK, HEAD)
        return sk[n - 8, :, hh].reshape(4 * LOCAL, HEAD)

    def values_of(hh, n):
        if n < 8:
            part = kv[pl.ds(hh * 32 + 4 * n, 4), 1]
            return part.reshape(4 * BLOCK, HEAD)
        return sv[n - 8, :, hh].reshape(4 * LOCAL, HEAD)

    spans = [(512 * n, 512) for n in range(8)] + [(4096, 256), (4352, 256)]

    def query_tile(t):
        hh, src = unit(t // 2)
        floats = qb[hh, src, pl.ds(pl.multiple_of((t % 2) * ROWS, ROWS), ROWS), :].astype(jnp.float32) * SCALE
        high = floats.astype(jnp.bfloat16)
        low = (floats - high.astype(jnp.float32)).astype(jnp.bfloat16)
        return jnp.concatenate([high, low], axis=1)

    def score(t, n, buf):
        hh, src = unit(t // 2)
        keys = keys_of(hh, n)
        first, size = spans[n]
        keys = jnp.concatenate([keys, keys], axis=1)
        s = lax.dot_general(query_tile(t), keys, NT, preferred_element_type=jnp.float32)
        if n >= 8:
            token = (2 * src + zh) * LOCAL + (t % 2) * (ROWS // GQ)
            row = token + lax.broadcasted_iota(jnp.int32, (ROWS, size), 0) // GQ
            col = lax.broadcasted_iota(jnp.int32, (ROWS, size), 1)
            col = (col // LOCAL) * (2 * LOCAL) + (n - 8) * LOCAL + col % LOCAL
            s = jnp.where(col <= row, s, -1e30)
        buf[:, first:first + size] = s
        top = s[:, :128]
        for j in range(1, size // 128):
            top = jnp.maximum(top, s[:, j * 128:(j + 1) * 128])
        return top

    def weigh(t, n, buf, top):
        hh, _ = unit(t // 2)
        first, size = spans[n]
        weights = jnp.exp2(buf[:, first:first + size] - top).astype(jnp.bfloat16)
        values = values_of(hh, n)
        values = jnp.concatenate([values, jnp.ones_like(values)], axis=1)
        return jnp.dot(weights, values, preferred_element_type=jnp.float32)

    def stage(tn, bufn, mn, tc, bufc, mc):
        top, total = None, None
        for n in range(len(spans)):
            if tc is None and n == 8:
                stretch_ready()
            if tn is not None:
                part = score(tn, n, bufn)
                top = part if top is None else jnp.maximum(top, part)
            if tc is not None:
                part = weigh(tc, n, bufc, mc[:, :1])
                total = part if total is None else total + part
        if tn is not None:
            mn[...] = jnp.broadcast_to(jnp.max(top, axis=1, keepdims=True), mn.shape)
        if tc is not None:
            hh, src = unit(tc // 2)
            result = (total[:, :HEAD] / total[:, HEAD:]).reshape(ROWS // GQ, GQ, HEAD)
            at = pl.ds(pl.multiple_of((tc % 2) * (ROWS // GQ), ROWS // GQ), ROWS // GQ)
            ob[hh, src, at] = result.astype(jnp.bfloat16)

    def result_copy(u):
        hh, src = unit(u)
        return pltpu.make_async_remote_copy(
            src_ref=ob.at[hh, src], dst_ref=out.at[:, 2 * y + hh],
            send_sem=osend.at[u], recv_sem=ro.at[hh, y],
            device_id={"outer": o, "inner": src * 2 + zh}, device_id_type=pl.DeviceIdType.MESH)

    def own_copy(u):
        hh, src = unit(u)
        return pltpu.make_async_copy(ob.at[hh, src], out.at[:, 2 * y + hh], osend.at[u])

    stage(0, sa, ma, None, None, None)

    def body(u, carry):
        stage(2 * u + 1, sb, mb, 2 * u, sa, ma)

        @pl.when((u < 6))
        def _():
            hh, src = unit(u + 1)
            got(qb.at[hh, src], rq.at[hh, src])

        @pl.when(u == 3)
        def _():
            for k in range(4):
                for dx in range(4):
                    s = slot(far(k), dx, 1)
                    got(kv.at[s], rs.at[s, 0])

        stage(jnp.minimum(2 * u + 2, 15), sa, ma, 2 * u + 1, sb, mb)

        @pl.when((u > 0) & (u < 7))
        def _():
            result_copy(u).start()

        @pl.when((u == 0) | (u == 7))
        def _():
            own_copy(u).start()

        @pl.when(u == 0)
        def _():
            relay(far(0))
            relay(far(1))

        @pl.when(u == 1)
        def _():
            relay(far(2))
            relay(far(3))

        @pl.when(u == 2)
        def _():
            for k in range(4):
                close(far(k))

        return carry

    lax.fori_loop(0, 8, body, 0)

    for wait in ends:
        wait()
    for u in range(8):
        if u in (0, 7):
            own_copy(u).wait()
        else:
            result_copy(u).wait_send()
    for hh in range(2):
        for d in (1, 2, 3):
            src = (y + d) % NY
            got(out.at[:, 2 * src + hh], ro.at[hh, src])


def shards(qkv, key_codes, codebooks, value_codes, value_scales, block_ids):
    block_rows = key_codes.shape[0]
    prefix_len = block_rows * lax.axis_size("outer")
    prefix_values = (value_codes.astype(jnp.float32) * value_scales[:, :, None]).astype(jnp.bfloat16)
    own_pos = block_ids[0] * block_rows + jnp.arange(block_rows, dtype=jnp.int32)
    prefix_keys = rotate(decode_block(key_codes, codebooks), own_pos).astype(jnp.bfloat16)
    kv_in = jnp.stack([prefix_keys[:, 0], prefix_values[:, 0]])
    stretch_pos = prefix_len + lax.axis_index("inner") * LOCAL + jnp.arange(LOCAL, dtype=jnp.int32)
    rotated = rotate(qkv[:, :, :GQ + 1], stretch_pos).astype(jnp.bfloat16)
    q_in = rotated[:, :, :GQ].transpose(1, 0, 2, 3).reshape(8, LOCAL * GQ, HEAD)
    sk_in = rotated[:, :, GQ].transpose(1, 0, 2)
    sv_in = qkv[:, :, GQ + 1].transpose(1, 0, 2)

    bf, f32 = jnp.bfloat16, jnp.float32
    dma = pltpu.SemaphoreType.DMA
    return pl.pallas_call(
        kernel,
        out_shape=jax.ShapeDtypeStruct((LOCAL, 8, GQ, HEAD), bf),
        in_specs=[pl.BlockSpec(memory_space=pltpu.VMEM)] * 4,
        out_specs=pl.BlockSpec(memory_space=pl.ANY),
        scratch_shapes=[
            pltpu.VMEM((64, 2, BLOCK, HEAD), bf),
            pltpu.VMEM((2, 4, LOCAL * GQ, HEAD), bf),
            pltpu.VMEM((2, 4, 2, LOCAL, HEAD), bf),
            pltpu.VMEM((2, 4, 2, LOCAL, HEAD), bf),
            pltpu.VMEM((4, 2, LOCAL, HEAD), bf),
            pltpu.VMEM((4, 2, LOCAL, HEAD), bf),
            pltpu.VMEM((2, 4, LOCAL, GQ, HEAD), bf),
            pltpu.VMEM((ROWS, 4608), f32),
            pltpu.VMEM((ROWS, 4608), f32),
            pltpu.VMEM((ROWS, 128), f32),
            pltpu.VMEM((ROWS, 128), f32),
            dma((128,)), dma((64, 2)), dma((2, 4)), dma((4,)), dma((4,)), dma((4,)), dma((4,)),
            dma((2,)), dma((2, 4)), dma((8,)), dma((8,)),
        ],
        compiler_params=pltpu.CompilerParams(
            collective_id=0, has_side_effects=True, vmem_limit_bytes=60 * 2**20),
    )(q_in, sk_in, sv_in, kv_in)


def solution(mesh):
    return jax.shard_map(
        shards,
        mesh=mesh,
        in_specs=(
            P(("outer", "inner"), None, None, None),
            P("outer", "inner", None),
            P("inner", None, None),
            P("outer", "inner", None),
            P("outer", "inner"),
            P("outer"),
        ),
        out_specs=P(("outer", "inner"), None, None, None),
        check_vma=False,
    )
```

```python
import functools
import math

import jax
import jax.numpy as jnp
import numpy as np
from jax import lax
from jax.experimental import pallas as pl
from jax.experimental.pallas import tpu as pltpu
from jax.sharding import PartitionSpec as P

rope_base = 500000.0
NX, NY, NZ, NH = 4, 4, 8, 4
BLOCK, HEAD, GQ, LOCAL, CODES, GROUPS, PREFIX = 128, 128, 8, 64, 256, 16, 4096
ROWS = 256
SCALE = 128**-0.5 * math.log2(math.e)
NT = (((1,), (1,)), ((), ()))
SPANS = [(512 * n, 512) for n in range(8)] + [(4096, 256), (4352, 256)]
WIDTH = 4608


def rope_tables():
    step = np.float32(-2.0 * math.log(rope_base) / HEAD)
    inverse = np.exp((np.arange(64, dtype=np.float32) * step).astype(np.float64)).astype(np.float32).astype(np.float64)
    inverse = np.concatenate([inverse, inverse])
    fine = np.arange(BLOCK)[:, None] * inverse
    starts = np.concatenate([np.arange(32) * BLOCK, PREFIX + np.arange(8) * LOCAL])
    coarse = starts[:, None] * inverse
    table = np.concatenate([np.cos(fine), np.sin(fine), np.cos(coarse), np.sin(coarse)])
    return jnp.asarray(table.astype(np.float32))


def kernel(qkv, codes, books, vcodes, scales, block, table, out,
           kv, qs, sks, svs, qb, sk, sv, ob, xs, cq, sq, g0, g1, mx,
           send, rs, rq, rsk, rsv, ro, loc, osend):
    o = lax.axis_index("outer")
    i = lax.axis_index("inner")
    zl, x, c = o // 8, (o // 2) % NX, o % 2
    y, zh = i // 2, i % 2

    def dev(dx=0, dy=0, dz=0, far=0, dc=0):
        outer = ((zl + dz) % NH) * 8 + ((x + dx) % NX) * 2 + (c + dc) % 2
        return {"outer": outer, "inner": ((y + dy) % NY) * 2 + (zh + far) % 2}

    peers = [dev(dz=d) for d in (1, 2, 3)] + [dev(dz=d, far=1) for d in range(4)]
    peers += [dev(dx=1), dev(dx=3), dev(dc=1)]
    peers += [dev(dy=d) for d in (1, 2, 3)] + [dev(dy=d, far=1) for d in (1, 2, 3)]
    barrier = pltpu.get_barrier_semaphore()
    for peer in peers:
        pl.semaphore_signal(barrier, inc=1, device_id=peer, device_id_type=pl.DeviceIdType.MESH)

    def slot(half, side, core, k):
        return ((half * 4 + side) * 2 + core) * 4 + k

    def angles(start, rows):
        fine_c, fine_s = table[:rows], table[BLOCK:BLOCK + rows]
        base_c = table[pl.ds(2 * BLOCK + start, 1), :]
        base_s = table[pl.ds(2 * BLOCK + 40 + start, 1), :]
        lane = lax.broadcasted_iota(jnp.int32, (rows, HEAD), 1)
        sine = base_s * fine_c + base_c * fine_s
        return base_c * fine_c - base_s * fine_s, jnp.where(lane < HEAD // 2, -sine, sine)

    book_t = books[...].astype(jnp.float32).T
    entry = lax.broadcasted_iota(jnp.int32, (CODES, BLOCK), 0)
    parts = []
    for g in range(GROUPS):
        hot = jnp.where(entry == codes[g:g + 1, :], 1.0, 0.0).astype(jnp.bfloat16)
        rows = book_t[8 * g:8 * g + 8, :].astype(jnp.bfloat16)
        parts.append(jnp.dot(rows, hot, preferred_element_type=jnp.float32))
    keys = jnp.concatenate(parts, axis=0).T
    cosine, sine = angles(block[0], BLOCK)
    own = slot(0, 0, 0, 0)
    kv[own, 0] = (keys * cosine + pltpu.roll(keys, HEAD // 2, 1) * sine).astype(jnp.bfloat16)
    scale = jnp.broadcast_to(scales[...], (BLOCK, BLOCK)).T
    kv[own, 1] = (vcodes[...].astype(jnp.float32) * scale).astype(jnp.bfloat16)
    cq[...], sq[...] = angles(32 + i, LOCAL)

    pl.semaphore_wait(barrier, len(peers))

    sent, ends = [], []
    likes = {r.shape: r for r in (kv.at[0], kv.at[0, 0], sks.at[pl.ds(0, 2)], qb.at[0, 0])}

    def put(src, dst, recv_sem, to):
        index = len(sent)
        sent.append(index)
        pltpu.make_async_remote_copy(
            src_ref=src, dst_ref=dst, send_sem=send.at[index], recv_sem=recv_sem,
            device_id=to, device_id_type=pl.DeviceIdType.MESH).start()
        like = likes[src.shape]
        ends.append(lambda: pltpu.make_async_copy(like, like, send.at[index]).wait())

    def got(dst, recv_sem):
        pltpu.make_async_copy(dst, dst, recv_sem).wait()

    kept = []

    def keep(src, dst):
        copy = pltpu.make_async_copy(src, dst, loc.at[len(kept)])
        copy.start()
        kept.append(copy)

    def full(half, side, core, k):
        s = slot(half, side, core, k)
        got(kv.at[s], rs.at[s, 0])

    def to_sides(half, k):
        src = kv.at[slot(half, 0, 0, k)]
        for side, dx in ((1, 1), (2, 3)):
            s = slot(half, side, 0, k)
            put(src, kv.at[s], rs.at[s, 0], dev(dx=dx))

    def to_core(half, side, k):
        s = slot(half, side, 1, k)
        put(kv.at[slot(half, side, 0, k)], kv.at[s], rs.at[s, 0], dev(dc=1))

    def relay(half, k):
        for side, dx in ((1, 1), (2, 3)):
            full(half, side, 0, k)
            s = slot(half, 3, 0, k)
            part = side - 1
            put(kv.at[slot(half, side, 0, k), part], kv.at[s, part], rs.at[s, part], dev(dx=dx))
            to_core(half, side, k)

    def close(half, k):
        s = slot(half, 3, 0, k)
        got(kv.at[s, 0], rs.at[s, 0])
        got(kv.at[s, 1], rs.at[s, 1])
        to_core(half, 3, k)

    to_sides(0, 0)
    for d in (1, 3, 2):
        s = slot(0, 0, 0, 4 - d)
        put(kv.at[own], kv.at[s], rs.at[s, 0], dev(dz=d))
    to_core(0, 0, 0)

    def turn(t, carry):
        rows = qkv[t].astype(jnp.float32)
        cosine, sine = cq[pl.ds(t, 1), :], sq[pl.ds(t, 1), :]
        head = rows[:9].reshape(72, HEAD)
        xs[pl.ds(pl.multiple_of(t * 80, 8), 72), :] = head * cosine + pltpu.roll(head, HEAD // 2, 1) * sine
        xs[pl.ds(pl.multiple_of(t * 80 + 72, 8), 8), :] = rows[9]
        return carry

    lax.fori_loop(0, LOCAL, turn, 0, unroll=4)
    for h in range(8):
        sks[h] = xs[pl.ds(64 + h, LOCAL, stride=80), :].astype(jnp.bfloat16)
        svs[h] = xs[pl.ds(72 + h, LOCAL, stride=80), :].astype(jnp.bfloat16)
    for d in range(4):
        pair = pl.ds(2 * ((y + d) % NY), 2)
        back = (4 - d) % 4
        put(sks.at[pair], sk.at[1, y], rsk.at[1, back], dev(dy=d, far=1))
        put(svs.at[pair], sv.at[1, y], rsv.at[1, back], dev(dy=d, far=1))
        if d == 0:
            keep(sks.at[pair], sk.at[0, y])
            keep(svs.at[pair], sv.at[0, y])
        else:
            put(sks.at[pair], sk.at[0, y], rsk.at[0, back], dev(dy=d))
            put(svs.at[pair], sv.at[0, y], rsv.at[0, back], dev(dy=d))

    def gather(t, carry):
        for h in range(8):
            two = [xs[pl.ds(t * 160 + 80 * j + h, 8, stride=8), :] for j in range(2)]
            qs[h, pl.ds(pl.multiple_of(t * 16, 16), 16), :] = jnp.concatenate(two, axis=0).astype(jnp.bfloat16)
        return carry

    lax.fori_loop(0, LOCAL // 2, gather, 0, unroll=2)
    for hr in range(2):
        for d in (0, 3, 1, 2):
            src = qs.at[2 * ((y + d) % NY) + (zh + hr) % 2]
            back = (4 - d) % 4
            if d == 0:
                keep(src, qb.at[hr, 0])
            else:
                put(src, qb.at[hr, back], rq.at[hr, back], dev(dy=d))
    for d in (0, 1, 3, 2):
        s = slot(1, 0, 0, (4 - d) % 4)
        put(kv.at[own], kv.at[s], rs.at[s, 0], dev(dz=d, far=1))

    def unit(u):
        k = min(u, 7 - u) if isinstance(u, int) else jnp.minimum(u, 7 - u)
        return u // 4, (k * (k + 1) // 2) % 4

    def token_block(hr, n, part):
        if n < 8:
            return kv[pl.ds(hr * 32 + 4 * n, 4), part].reshape(4 * BLOCK, HEAD)
        ref = sk if part == 0 else sv
        return ref[n - 8, :, (zh + hr) % 2].reshape(4 * LOCAL, HEAD)

    def query_tile(t):
        hr, d = unit(t // 2)
        floats = qb[hr, d, pl.ds(pl.multiple_of((t % 2) * ROWS, ROWS), ROWS), :].astype(jnp.float32) * SCALE
        high = floats.astype(jnp.bfloat16)
        low = (floats - high.astype(jnp.float32)).astype(jnp.bfloat16)
        return jnp.concatenate([high, low], axis=1)

    def score(t, n, buf, j):
        hr, d = unit(t // 2)
        keys = token_block(hr, n, 0)
        first, size = SPANS[n]
        keys = jnp.concatenate([keys, keys], axis=1)
        s = lax.dot_general(query_tile(t), keys, NT, preferred_element_type=jnp.float32)
        if n >= 8:
            token = (2 * ((y + d) % NY) + zh) * LOCAL + (t % 2) * (ROWS // GQ)
            row = token + lax.broadcasted_iota(jnp.int32, (ROWS, size), 0) // GQ
            col = lax.broadcasted_iota(jnp.int32, (ROWS, size), 1)
            col = (col // LOCAL) * (2 * LOCAL) + ((zh + n) % 2) * LOCAL + col % LOCAL
            s = jnp.where(col <= row, s, -1e30)
        buf[j, :, first:first + size] = s
        top = s[:, :128]
        for m in range(1, size // 128):
            top = jnp.maximum(top, s[:, m * 128:(m + 1) * 128])
        return top

    def weigh(t, n, buf, j, top):
        hr, _ = unit(t // 2)
        first, size = SPANS[n]
        weights = jnp.exp2(buf[j, :, first:first + size] - top).astype(jnp.bfloat16)
        values = token_block(hr, n, 1)
        values = jnp.concatenate([values, jnp.ones_like(values)], axis=1)
        return jnp.dot(weights, values, preferred_element_type=jnp.float32)

    def widest(top):
        return jnp.broadcast_to(jnp.max(top, axis=1, keepdims=True), (ROWS, 128))

    def stage(t, buf, j, tn=None, bufn=None):
        top, total = None, None
        peak = mx[t % 8][:, :1]
        for n in range(len(SPANS)):
            if tn is not None:
                part = score(tn, n, bufn, j)
                top = part if top is None else jnp.maximum(top, part)
            part = weigh(t, n, buf, j, peak)
            total = part if total is None else total + part
        if tn is not None:
            mx[tn % 8] = widest(top)
        hr, d = unit(t // 2)
        result = (total[:, :HEAD] / total[:, HEAD:]).reshape(ROWS // GQ, GQ, HEAD)
        at = pl.ds(pl.multiple_of((t % 2) * (ROWS // GQ), ROWS // GQ), ROWS // GQ)
        ob[hr, d, at] = result.astype(jnp.bfloat16)

    def head_of(hr):
        return 2 * y + (zh + hr) % 2

    def result_copy(u):
        hr, d = unit(u)
        return pltpu.make_async_remote_copy(
            src_ref=ob.at[hr, d], dst_ref=out.at[:, head_of(hr)],
            send_sem=osend.at[u], recv_sem=ro.at[hr, (4 - d) % 4],
            device_id=dev(dy=d), device_id_type=pl.DeviceIdType.MESH)

    def own_copy(u):
        hr, d = unit(u)
        return pltpu.make_async_copy(ob.at[hr, d], out.at[:, head_of(hr)], osend.at[u])

    def deliver(t):
        @pl.when((t % 2 == 1) & (t != 1) & (t != 15))
        def _():
            result_copy(t // 2).start()

        @pl.when((t == 1) | (t == 15))
        def _():
            own_copy(t // 2).start()

    def early(n, first=False):
        def two(j, carry):
            for half, buf in ((0, g0), (1, g1)):
                t = 4 * half + j
                part = score(t, n, buf, j)
                mx[t] = part if first else jnp.maximum(mx[t], part)
            return carry
        lax.fori_loop(0, 4, two, 0)

    first = (zl == 0).astype(jnp.int32)
    last = (zl == NH - 1).astype(jnp.int32)
    ka = 1 + 2 * last
    kb = 3 - first - last
    near = (0, ka, kb, 6 - ka - kb)
    for n in (1, 2, 3):
        full(0, 0, 0, near[n])
        to_sides(0, near[n])
        to_core(0, 0, near[n])
        relay(0, near[n - 1])
    for copy in kept:
        copy.wait()
    for d in (1, 3, 2):
        got(qb.at[0, d], rq.at[0, d])
    early(0, True)
    relay(0, near[3])
    for n in range(4):
        full(0, 0, 1, n)
    early(1)
    for n in range(4):
        close(0, near[n])
    early(2)
    early(4)
    for n in range(4):
        full(1, 0, 0, n)
        to_sides(1, n)
        to_core(1, 0, n)
    for n in range(4):
        full(0, 1, 1, n)
        full(0, 2, 1, n)
    early(3)
    early(5)
    early(6)
    for n in range(4):
        full(0, 3, 1, n)
    early(7)
    for d in range(4):
        for zr in range(2):
            if d > 0 or zr > 0:
                src = (y + d) % NY
                got(sk.at[zr, src], rsk.at[zr, d])
                got(sv.at[zr, src], rsv.at[zr, d])
    early(8)
    early(9)
    for t in range(8):
        mx[t] = widest(mx[t])

    def loop(start, step):
        def body(j, carry):
            step(j)
            deliver(start + j)
            return carry
        lax.fori_loop(0, 4, body, 0)

    def opening(j):
        stage(j, g0, j)

        @pl.when(j == 0)
        def _():
            relay(1, 0)
            relay(1, 1)

        @pl.when(j == 1)
        def _():
            relay(1, 2)
            relay(1, 3)

        @pl.when(j == 3)
        def _():
            for n in range(4):
                close(1, n)

    loop(0, opening)
    for side in range(4):
        for n in range(4):
            full(1, side, 1, n)
    for d in (1, 3, 2):
        got(qb.at[1, d], rq.at[1, d])
    loop(4, lambda j: stage(4 + j, g1, j, 8 + j, g0))
    loop(8, lambda j: stage(8 + j, g0, j, 12 + j, g1))
    loop(12, lambda j: stage(12 + j, g1, j))

    for wait in ends:
        wait()
    for u in range(8):
        if u in (0, 7):
            own_copy(u).wait()
        else:
            result_copy(u).wait_send()
    for hr in range(2):
        for d in (1, 2, 3):
            got(out.at[:, 2 * ((y + d) % NY) + (zh + hr) % 2], ro.at[hr, d])


def shards(qkv, key_codes, codebooks, value_codes, value_scales, block_ids):
    bf, f32 = jnp.bfloat16, jnp.float32
    dma = pltpu.SemaphoreType.DMA
    vmem = pl.BlockSpec(memory_space=pltpu.VMEM)
    return pl.pallas_call(
        kernel,
        out_shape=jax.ShapeDtypeStruct((LOCAL, 8, GQ, HEAD), bf),
        in_specs=[vmem] * 5 + [pl.BlockSpec(memory_space=pltpu.SMEM), vmem],
        out_specs=pl.BlockSpec(memory_space=pl.ANY),
        scratch_shapes=[
            pltpu.VMEM((64, 2, BLOCK, HEAD), bf),
            pltpu.VMEM((8, LOCAL * GQ, HEAD), bf),
            pltpu.VMEM((8, LOCAL, HEAD), bf),
            pltpu.VMEM((8, LOCAL, HEAD), bf),
            pltpu.VMEM((2, 4, LOCAL * GQ, HEAD), bf),
            pltpu.VMEM((2, 4, 2, LOCAL, HEAD), bf),
            pltpu.VMEM((2, 4, 2, LOCAL, HEAD), bf),
            pltpu.VMEM((2, 4, LOCAL, GQ, HEAD), bf),
            pltpu.VMEM((LOCAL * 80, HEAD), f32),
            pltpu.VMEM((LOCAL, HEAD), f32),
            pltpu.VMEM((LOCAL, HEAD), f32),
            pltpu.VMEM((4, ROWS, WIDTH), f32),
            pltpu.VMEM((4, ROWS, WIDTH), f32),
            pltpu.VMEM((8, ROWS, 128), f32),
            dma((128,)), dma((64, 2)), dma((2, 4)), dma((2, 4)), dma((2, 4)),
            dma((2, 4)), dma((8,)), dma((8,)),
        ],
        compiler_params=pltpu.CompilerParams(
            collective_id=0, has_side_effects=True, vmem_limit_bytes=60 * 2**20),
    )(qkv.transpose(0, 2, 1, 3), key_codes[:, 0].T, codebooks[0], value_codes[:, 0],
      value_scales.T, block_ids, rope_tables())


def solution(mesh):
    return jax.shard_map(
        shards,
        mesh=mesh,
        in_specs=(
            P(("outer", "inner"), None, None, None),
            P("outer", "inner", None),
            P("inner", None, None),
            P("outer", "inner", None),
            P("outer", "inner"),
            P("outer"),
        ),
        out_specs=P(("outer", "inner"), None, None, None),
        check_vma=False,
    )
```

```python
import functools
import math

import jax
import jax.numpy as jnp
import numpy as np
from jax import lax
from jax.experimental import pallas as pl
from jax.experimental.pallas import tpu as pltpu
from jax.sharding import PartitionSpec as P

rope_base = 500000.0
NX, NY, NZ, NH = 4, 4, 8, 4
BLOCK, HEAD, GQ, LOCAL, CODES, GROUPS, PREFIX = 128, 128, 8, 64, 256, 16, 4096
ROWS = 256
SCALE = 128**-0.5 * math.log2(math.e)
NT = (((1,), (1,)), ((), ()))
SPANS = [(512 * n, 512) for n in range(8)] + [(4096, 256), (4352, 256)]
WIDTH = 4608


def rope_tables():
    step = np.float32(-2.0 * math.log(rope_base) / HEAD)
    inverse = np.exp((np.arange(64, dtype=np.float32) * step).astype(np.float64)).astype(np.float32).astype(np.float64)
    inverse = np.concatenate([inverse, inverse])
    fine = np.arange(BLOCK)[:, None] * inverse
    starts = np.concatenate([np.arange(32) * BLOCK, PREFIX + np.arange(8) * LOCAL])
    coarse = starts[:, None] * inverse
    table = np.concatenate([np.cos(fine), np.sin(fine), np.cos(coarse), np.sin(coarse)])
    return jnp.asarray(table.astype(np.float32))


def kernel(qkv, codes, books, vcodes, scales, block, table, out,
           kv, qs, sks, svs, qb, sk, sv, rk, rv, ob, xs, cq, sq, g0, g1, mx,
           send, rs, rq, rsk, rsv, ro, loc, osend):
    o = lax.axis_index("outer")
    i = lax.axis_index("inner")
    zl, x, c = o // 8, (o // 2) % NX, o % 2
    y, zh = i // 2, i % 2
    z = zh * NH + zl

    def dev(dx=0, dy=0, dz=0, dc=0):
        z1 = (z + dz) % NZ
        outer = (z1 % NH) * 8 + ((x + dx) % NX) * 2 + (c + dc) % 2
        return {"outer": outer, "inner": ((y + dy) % NY) * 2 + z1 // NH}

    peers = [dev(dz=d) for d in (1, -1, 2, -2)] + [dev(dx=1), dev(dx=3), dev(dc=1)]
    peers += [dev(dy=d) for d in (1, 2, 3)]
    barrier = pltpu.get_barrier_semaphore()
    for peer in peers:
        pl.semaphore_signal(barrier, inc=1, device_id=peer, device_id_type=pl.DeviceIdType.MESH)

    def slot(half, side, core, k):
        return ((half * 4 + side) * 2 + core) * 4 + k

    def z_slot(src, at=0):
        half = (((z + src) % NZ) // NH + ((z + at) % NZ) // NH) % 2
        return slot(half, 0, 0, (src - at) % 4)

    def angles(start, rows):
        fine_c, fine_s = table[:rows], table[BLOCK:BLOCK + rows]
        base_c = table[pl.ds(2 * BLOCK + start, 1), :]
        base_s = table[pl.ds(2 * BLOCK + 40 + start, 1), :]
        lane = lax.broadcasted_iota(jnp.int32, (rows, HEAD), 1)
        sine = base_s * fine_c + base_c * fine_s
        return base_c * fine_c - base_s * fine_s, jnp.where(lane < HEAD // 2, -sine, sine)

    book_t = books[...].astype(jnp.float32).T
    entry = lax.broadcasted_iota(jnp.int32, (CODES, BLOCK), 0)
    parts = []
    for g in range(GROUPS):
        hot = jnp.where(entry == codes[g:g + 1, :], 1.0, 0.0).astype(jnp.bfloat16)
        rows = book_t[8 * g:8 * g + 8, :].astype(jnp.bfloat16)
        parts.append(jnp.dot(rows, hot, preferred_element_type=jnp.float32))
    keys = jnp.concatenate(parts, axis=0).T
    cosine, sine = angles(block[0], BLOCK)
    own = slot(0, 0, 0, 0)
    kv[own, 0] = (keys * cosine + pltpu.roll(keys, HEAD // 2, 1) * sine).astype(jnp.bfloat16)
    scale = jnp.broadcast_to(scales[...], (BLOCK, BLOCK)).T
    kv[own, 1] = (vcodes[...].astype(jnp.float32) * scale).astype(jnp.bfloat16)
    cq[...], sq[...] = angles(32 + i, LOCAL)

    pl.semaphore_wait(barrier, len(peers))

    sent, ends = [], []
    likes = {r.shape: r for r in (kv.at[0], kv.at[0, 0], sks.at[pl.ds(0, 2)], qb.at[0, 0], rk)}

    def put(src, dst, recv_sem, to):
        index = len(sent)
        sent.append(index)
        pltpu.make_async_remote_copy(
            src_ref=src, dst_ref=dst, send_sem=send.at[index], recv_sem=recv_sem,
            device_id=to, device_id_type=pl.DeviceIdType.MESH).start()
        like = likes[src.shape]
        ends.append(lambda: pltpu.make_async_copy(like, like, send.at[index]).wait())

    def got(dst, recv_sem):
        pltpu.make_async_copy(dst, dst, recv_sem).wait()

    kept = []

    def keep(src, dst):
        copy = pltpu.make_async_copy(src, dst, loc.at[len(kept)])
        copy.start()
        kept.append(copy)

    def full(half, side, core, k):
        s = slot(half, side, core, k)
        got(kv.at[s], rs.at[s, 0])

    def to_sides(half, k):
        src = kv.at[slot(half, 0, 0, k)]
        for side, dx in ((1, 1), (2, 3)):
            s = slot(half, side, 0, k)
            put(src, kv.at[s], rs.at[s, 0], dev(dx=dx))

    def to_core(half, side, k):
        s = slot(half, side, 1, k)
        put(kv.at[slot(half, side, 0, k)], kv.at[s], rs.at[s, 0], dev(dc=1))

    def relay(half, k):
        for side, dx in ((1, 1), (2, 3)):
            full(half, side, 0, k)
            s = slot(half, 3, 0, k)
            part = side - 1
            put(kv.at[slot(half, side, 0, k), part], kv.at[s, part], rs.at[s, part], dev(dx=dx))
            to_core(half, side, k)

    def close(half, k):
        s = slot(half, 3, 0, k)
        got(kv.at[s, 0], rs.at[s, 0])
        got(kv.at[s, 1], rs.at[s, 1])
        to_core(half, 3, k)

    def along_z(src, at):
        s = z_slot(src, at)
        put(kv.at[z_slot(src)], kv.at[s], rs.at[s, 0], dev(dz=at))

    def half_along_z(src, at, part):
        s = z_slot(src, at)
        put(kv.at[z_slot(src), part], kv.at[s, part], rs.at[s, part], dev(dz=at))

    def from_z(src):
        s = z_slot(src)
        got(kv.at[s], rs.at[s, 0])

    for d in (1, -1, 2, -2):
        along_z(0, d)
    to_sides(0, 0)
    to_core(0, 0, 0)

    def turn(t, carry):
        rows = qkv[t].astype(jnp.float32)
        cosine, sine = cq[pl.ds(t, 1), :], sq[pl.ds(t, 1), :]
        head = rows[:9].reshape(72, HEAD)
        xs[pl.ds(pl.multiple_of(t * 80, 8), 72), :] = head * cosine + pltpu.roll(head, HEAD // 2, 1) * sine
        xs[pl.ds(pl.multiple_of(t * 80 + 72, 8), 8), :] = rows[9]
        return carry

    lax.fori_loop(0, LOCAL, turn, 0, unroll=4)
    for h in range(8):
        sks[h] = xs[pl.ds(64 + h, LOCAL, stride=80), :].astype(jnp.bfloat16)
        svs[h] = xs[pl.ds(72 + h, LOCAL, stride=80), :].astype(jnp.bfloat16)
    for d in range(4):
        pair = pl.ds(2 * ((y + d) % NY), 2)
        back = (4 - d) % 4
        if d == 0:
            keep(sks.at[pair], sk.at[0, y])
            keep(svs.at[pair], sv.at[0, y])
        else:
            put(sks.at[pair], sk.at[0, y], rsk.at[0, back], dev(dy=d))
            put(svs.at[pair], sv.at[0, y], rsv.at[0, back], dev(dy=d))

    def gather(t, carry):
        for h in range(8):
            two = [xs[pl.ds(t * 160 + 80 * j + h, 8, stride=8), :] for j in range(2)]
            qs[h, pl.ds(pl.multiple_of(t * 16, 16), 16), :] = jnp.concatenate(two, axis=0).astype(jnp.bfloat16)
        return carry

    lax.fori_loop(0, LOCAL // 2, gather, 0, unroll=2)
    for hr in range(2):
        for d in (0, 3, 1, 2):
            src = qs.at[2 * ((y + d) % NY) + (zh + hr) % 2]
            back = (4 - d) % 4
            if d == 0:
                keep(src, qb.at[hr, 0])
            else:
                put(src, qb.at[hr, back], rq.at[hr, back], dev(dy=d))

    def unit(u):
        k = min(u, 7 - u) if isinstance(u, int) else jnp.minimum(u, 7 - u)
        return u // 4, (k * (k + 1) // 2) % 4

    def token_block(hr, n, part):
        if n < 8:
            return kv[pl.ds(hr * 32 + 4 * n, 4), part].reshape(4 * BLOCK, HEAD)
        ref = sk if part == 0 else sv
        return ref[n - 8, :, (zh + hr) % 2].reshape(4 * LOCAL, HEAD)

    def query_tile(t):
        hr, d = unit(t // 2)
        floats = qb[hr, d, pl.ds(pl.multiple_of((t % 2) * ROWS, ROWS), ROWS), :].astype(jnp.float32) * SCALE
        high = floats.astype(jnp.bfloat16)
        low = (floats - high.astype(jnp.float32)).astype(jnp.bfloat16)
        return jnp.concatenate([high, low], axis=1)

    def score(t, n, buf, j):
        hr, d = unit(t // 2)
        keys = token_block(hr, n, 0)
        first, size = SPANS[n]
        keys = jnp.concatenate([keys, keys], axis=1)
        s = lax.dot_general(query_tile(t), keys, NT, preferred_element_type=jnp.float32)
        if n >= 8:
            token = (2 * ((y + d) % NY) + zh) * LOCAL + (t % 2) * (ROWS // GQ)
            row = token + lax.broadcasted_iota(jnp.int32, (ROWS, size), 0) // GQ
            col = lax.broadcasted_iota(jnp.int32, (ROWS, size), 1)
            col = (col // LOCAL) * (2 * LOCAL) + ((zh + n) % 2) * LOCAL + col % LOCAL
            s = jnp.where(col <= row, s, -1e30)
        buf[j, :, first:first + size] = s
        top = s[:, :128]
        for m in range(1, size // 128):
            top = jnp.maximum(top, s[:, m * 128:(m + 1) * 128])
        return top

    def weigh(t, n, buf, j, top):
        hr, _ = unit(t // 2)
        first, size = SPANS[n]
        weights = jnp.exp2(buf[j, :, first:first + size] - top).astype(jnp.bfloat16)
        values = token_block(hr, n, 1)
        values = jnp.concatenate([values, jnp.ones_like(values)], axis=1)
        return jnp.dot(weights, values, preferred_element_type=jnp.float32)

    def widest(top):
        return jnp.broadcast_to(jnp.max(top, axis=1, keepdims=True), (ROWS, 128))

    def stage(t, buf, j, tn=None, bufn=None):
        top, total = None, None
        peak = mx[t % 8][:, :1]
        for n in range(len(SPANS)):
            if tn is not None:
                part = score(tn, n, bufn, j)
                top = part if top is None else jnp.maximum(top, part)
            part = weigh(t, n, buf, j, peak)
            total = part if total is None else total + part
        if tn is not None:
            mx[tn % 8] = widest(top)
        hr, d = unit(t // 2)
        result = (total[:, :HEAD] / total[:, HEAD:]).reshape(ROWS // GQ, GQ, HEAD)
        at = pl.ds(pl.multiple_of((t % 2) * (ROWS // GQ), ROWS // GQ), ROWS // GQ)
        ob[hr, d, at] = result.astype(jnp.bfloat16)

    def head_of(hr):
        return 2 * y + (zh + hr) % 2

    def result_copy(u):
        hr, d = unit(u)
        return pltpu.make_async_remote_copy(
            src_ref=ob.at[hr, d], dst_ref=out.at[:, head_of(hr)],
            send_sem=osend.at[u], recv_sem=ro.at[hr, (4 - d) % 4],
            device_id=dev(dy=d), device_id_type=pl.DeviceIdType.MESH)

    def own_copy(u):
        hr, d = unit(u)
        return pltpu.make_async_copy(ob.at[hr, d], out.at[:, head_of(hr)], osend.at[u])

    def deliver(t):
        @pl.when((t % 2 == 1) & (t != 1) & (t != 15))
        def _():
            result_copy(t // 2).start()

        @pl.when((t == 1) | (t == 15))
        def _():
            own_copy(t // 2).start()

    def early(n, first=False):
        def two(j, carry):
            for half, buf in ((0, g0), (1, g1)):
                t = 4 * half + j
                part = score(t, n, buf, j)
                mx[t] = part if first else jnp.maximum(mx[t], part)
            return carry
        lax.fori_loop(0, 4, two, 0, unroll=True)

    first = (zl == 0).astype(jnp.int32)
    last = (zl == NH - 1).astype(jnp.int32)
    ka = 1 + 2 * last
    kb = 3 - first - last
    near = (0, ka, kb, 6 - ka - kb)
    def spread(half, k):
        to_sides(half, k)
        to_core(half, 0, k)

    from_z(-1)
    from_z(1)
    spread(0, near[1])
    for sign in (-1, 1):
        from_z(2 * sign)
        along_z(2 * sign, -sign)
    spread(0, near[2])
    relay(0, near[0])
    for sign in (-1, 1):
        from_z(3 * sign)
        half_along_z(3 * sign, -sign, (1 + sign) // 2)
    spread(0, near[3])
    for copy in kept[:2]:
        copy.wait()
    for d in (1, 2, 3):
        src = (y + d) % NY
        got(sk.at[0, src], rsk.at[0, d])
        got(sv.at[0, src], rsv.at[0, d])
    put(sk.at[0], rk, rsk.at[1, 0], dev(dz=2))
    put(sv.at[0], rv, rsv.at[1, 0], dev(dz=-2))
    relay(0, near[1])
    for copy in kept[2:]:
        copy.wait()
    for d in (1, 3, 2):
        got(qb.at[0, d], rq.at[0, d])
    early(0, True)
    relay(0, near[2])
    s = slot(1, 0, 0, 0)
    got(kv.at[s, 0], rs.at[s, 0])
    got(kv.at[s, 1], rs.at[s, 1])
    relay(0, near[3])
    got(rk, rsk.at[1, 0])
    put(rk, sk.at[1], rsk.at[1, 1], dev(dz=2))
    got(rv, rsv.at[1, 0])
    put(rv, sv.at[1], rsv.at[1, 1], dev(dz=-2))
    for n in range(4):
        spread(1, n)
    for n in range(4):
        full(0, 0, 1, n)
    early(1)
    for n in range(4):
        close(0, near[n])
    early(2)
    early(4)
    for n in range(4):
        full(0, 1, 1, n)
        full(0, 2, 1, n)
    early(3)
    early(5)
    early(6)
    for n in range(4):
        full(0, 3, 1, n)
    early(7)
    got(sk.at[1], rsk.at[1, 1])
    got(sv.at[1], rsv.at[1, 1])
    early(8)
    early(9)
    for t in range(8):
        mx[t] = widest(mx[t])

    def loop(start, step):
        def body(j, carry):
            step(j)
            deliver(start + j)
            return carry
        lax.fori_loop(0, 4, body, 0)

    def opening(j):
        stage(j, g0, j)

        @pl.when(j == 0)
        def _():
            relay(1, 0)
            relay(1, 1)

        @pl.when(j == 1)
        def _():
            relay(1, 2)
            relay(1, 3)

        @pl.when(j == 3)
        def _():
            for n in range(4):
                close(1, n)

    loop(0, opening)
    for side in range(4):
        for n in range(4):
            full(1, side, 1, n)
    for d in (1, 3, 2):
        got(qb.at[1, d], rq.at[1, d])
    loop(4, lambda j: stage(4 + j, g1, j, 8 + j, g0))
    loop(8, lambda j: stage(8 + j, g0, j, 12 + j, g1))
    loop(12, lambda j: stage(12 + j, g1, j))

    for wait in ends:
        wait()
    for u in range(8):
        if u in (0, 7):
            own_copy(u).wait()
        else:
            result_copy(u).wait_send()
    for hr in range(2):
        for d in (1, 2, 3):
            got(out.at[:, 2 * ((y + d) % NY) + (zh + hr) % 2], ro.at[hr, d])


def shards(qkv, key_codes, codebooks, value_codes, value_scales, block_ids):
    bf, f32 = jnp.bfloat16, jnp.float32
    dma = pltpu.SemaphoreType.DMA
    vmem = pl.BlockSpec(memory_space=pltpu.VMEM)
    return pl.pallas_call(
        kernel,
        out_shape=jax.ShapeDtypeStruct((LOCAL, 8, GQ, HEAD), bf),
        in_specs=[vmem] * 5 + [pl.BlockSpec(memory_space=pltpu.SMEM), vmem],
        out_specs=pl.BlockSpec(memory_space=pl.ANY),
        scratch_shapes=[
            pltpu.VMEM((64, 2, BLOCK, HEAD), bf),
            pltpu.VMEM((8, LOCAL * GQ, HEAD), bf),
            pltpu.VMEM((8, LOCAL, HEAD), bf),
            pltpu.VMEM((8, LOCAL, HEAD), bf),
            pltpu.VMEM((2, 4, LOCAL * GQ, HEAD), bf),
            pltpu.VMEM((2, 4, 2, LOCAL, HEAD), bf),
            pltpu.VMEM((2, 4, 2, LOCAL, HEAD), bf),
            pltpu.VMEM((4, 2, LOCAL, HEAD), bf),
            pltpu.VMEM((4, 2, LOCAL, HEAD), bf),
            pltpu.VMEM((2, 4, LOCAL, GQ, HEAD), bf),
            pltpu.VMEM((LOCAL * 80, HEAD), f32),
            pltpu.VMEM((LOCAL, HEAD), f32),
            pltpu.VMEM((LOCAL, HEAD), f32),
            pltpu.VMEM((4, ROWS, WIDTH), f32),
            pltpu.VMEM((4, ROWS, WIDTH), f32),
            pltpu.VMEM((8, ROWS, 128), f32),
            dma((128,)), dma((64, 2)), dma((2, 4)), dma((2, 4)), dma((2, 4)),
            dma((2, 4)), dma((8,)), dma((8,)),
        ],
        compiler_params=pltpu.CompilerParams(
            collective_id=0, has_side_effects=True, vmem_limit_bytes=60 * 2**20),
    )(qkv.transpose(0, 2, 1, 3), key_codes[:, 0].T, codebooks[0], value_codes[:, 0],
      value_scales.T, block_ids, rope_tables())


def solution(mesh):
    return jax.shard_map(
        shards,
        mesh=mesh,
        in_specs=(
            P(("outer", "inner"), None, None, None),
            P("outer", "inner", None),
            P("inner", None, None),
            P("outer", "inner", None),
            P("outer", "inner"),
            P("outer"),
        ),
        out_specs=P(("outer", "inner"), None, None, None),
        check_vma=False,
    )
```

```python
import functools
import math

import jax
import jax.numpy as jnp
import numpy as np
from jax import lax
from jax.experimental import pallas as pl
from jax.experimental.pallas import tpu as pltpu
from jax.sharding import PartitionSpec as P

rope_base = 500000.0
NX, NY, NZ, NH = 4, 4, 8, 4
BLOCK, HEAD, GQ, LOCAL, CODES, GROUPS, PREFIX = 128, 128, 8, 64, 256, 16, 4096
ROWS = 256
SCALE = 128**-0.5 * math.log2(math.e)
NT = (((1,), (1,)), ((), ()))
SPANS = [(512 * n, 512) for n in range(8)] + [(4096, 256), (4352, 256)]
WIDTH = 4608
DIRECT = (1, 0)


def rope_tables():
    step = np.float32(-2.0 * math.log(rope_base) / HEAD)
    inverse = np.exp((np.arange(64, dtype=np.float32) * step).astype(np.float64)).astype(np.float32).astype(np.float64)
    inverse = np.concatenate([inverse, inverse])
    fine = np.arange(BLOCK)[:, None] * inverse
    starts = np.concatenate([np.arange(32) * BLOCK, PREFIX + np.arange(8) * LOCAL])
    coarse = starts[:, None] * inverse
    table = np.concatenate([np.cos(fine), np.sin(fine), np.cos(coarse), np.sin(coarse)])
    return jnp.asarray(table.astype(np.float32))


def kernel(raw, codes, books, vcodes, scales, block, table, out,
           qkv, kv, qs, sks, svs, qb, sk, sv, rk, rv, ob, xs, cq, sq, g0, g1, mx,
           send, rs, rq, rsk, rsv, ro, loc, osend, load):
    o = lax.axis_index("outer")
    i = lax.axis_index("inner")
    zl, x, c = o // 8, (o // 2) % NX, o % 2
    y, zh = i // 2, i % 2
    z = zh * NH + zl

    def dev(dx=0, dy=0, dz=0, dc=0):
        z1 = (z + dz) % NZ
        outer = (z1 % NH) * 8 + ((x + dx) % NX) * 2 + (c + dc) % 2
        return {"outer": outer, "inner": ((y + dy) % NY) * 2 + z1 // NH}

    peers = [dev(dz=d) for d in (1, -1, 2, -2)] + [dev(dx=d) for d in (1, 2, 3)] + [dev(dc=1)]
    peers += [dev(dy=d) for d in (1, 2, 3)]
    barrier = pltpu.get_barrier_semaphore()
    for peer in peers:
        pl.semaphore_signal(barrier, inc=1, device_id=peer, device_id_type=pl.DeviceIdType.MESH)

    loading = pltpu.make_async_copy(raw, qkv, load)
    loading.start()

    def slot(half, side, core, k):
        return ((half * 4 + side) * 2 + core) * 4 + k

    def z_slot(src, at=0):
        half = (((z + src) % NZ) // NH + ((z + at) % NZ) // NH) % 2
        return slot(half, 0, 0, (src - at) % 4)

    def angles(start, rows):
        fine_c, fine_s = table[:rows], table[BLOCK:BLOCK + rows]
        base_c = table[pl.ds(2 * BLOCK + start, 1), :]
        base_s = table[pl.ds(2 * BLOCK + 40 + start, 1), :]
        lane = lax.broadcasted_iota(jnp.int32, (rows, HEAD), 1)
        sine = base_s * fine_c + base_c * fine_s
        return base_c * fine_c - base_s * fine_s, jnp.where(lane < HEAD // 2, -sine, sine)

    book_t = books[...].astype(jnp.float32).T
    entry = lax.broadcasted_iota(jnp.int32, (CODES, BLOCK), 0)
    parts = []
    for g in range(GROUPS):
        hot = jnp.where(entry == codes[g:g + 1, :], 1.0, 0.0).astype(jnp.bfloat16)
        rows = book_t[8 * g:8 * g + 8, :].astype(jnp.bfloat16)
        parts.append(jnp.dot(rows, hot, preferred_element_type=jnp.float32))
    keys = jnp.concatenate(parts, axis=0).T
    cosine, sine = angles(block[0], BLOCK)
    own = slot(0, 0, 0, 0)
    kv[own, 0] = (keys * cosine + pltpu.roll(keys, HEAD // 2, 1) * sine).astype(jnp.bfloat16)
    scale = jnp.broadcast_to(scales[...], (BLOCK, BLOCK)).T
    kv[own, 1] = (vcodes[...].astype(jnp.float32) * scale).astype(jnp.bfloat16)
    cq[...], sq[...] = angles(32 + i, LOCAL)

    pl.semaphore_wait(barrier, len(peers))

    sent, ends = [], []
    likes = {r.shape: r for r in (kv.at[0], kv.at[0, 0], sks.at[pl.ds(0, 2)], qb.at[0, 0], rk)}

    def put(src, dst, recv_sem, to):
        index = len(sent)
        sent.append(index)
        pltpu.make_async_remote_copy(
            src_ref=src, dst_ref=dst, send_sem=send.at[index], recv_sem=recv_sem,
            device_id=to, device_id_type=pl.DeviceIdType.MESH).start()
        like = likes[src.shape]
        ends.append(lambda: pltpu.make_async_copy(like, like, send.at[index]).wait())

    def got(dst, recv_sem):
        pltpu.make_async_copy(dst, dst, recv_sem).wait()

    kept = []

    def keep(src, dst):
        copy = pltpu.make_async_copy(src, dst, loc.at[len(kept)])
        copy.start()
        kept.append(copy)

    def full(half, side, core, k):
        s = slot(half, side, core, k)
        got(kv.at[s], rs.at[s, 0])

    def to_sides(half, k):
        src = kv.at[slot(half, 0, 0, k)]
        for side, dx in ((1, 1), (2, 3), (3, 2))[:2 + DIRECT[half]]:
            s = slot(half, side, 0, k)
            put(src, kv.at[s], rs.at[s, 0], dev(dx=dx))

    def to_core(half, side, k):
        s = slot(half, side, 1, k)
        put(kv.at[slot(half, side, 0, k)], kv.at[s], rs.at[s, 0], dev(dc=1))

    def relay(half, k):
        for side, dx in ((1, 1), (2, 3)):
            full(half, side, 0, k)
            s = slot(half, 3, 0, k)
            part = side - 1
            if not DIRECT[half]:
                put(kv.at[slot(half, side, 0, k), part], kv.at[s, part], rs.at[s, part], dev(dx=dx))
            to_core(half, side, k)

    def close(half, k):
        s = slot(half, 3, 0, k)
        if DIRECT[half]:
            got(kv.at[s], rs.at[s, 0])
        else:
            got(kv.at[s, 0], rs.at[s, 0])
            got(kv.at[s, 1], rs.at[s, 1])
        to_core(half, 3, k)

    def along_z(src, at):
        s = z_slot(src, at)
        put(kv.at[z_slot(src)], kv.at[s], rs.at[s, 0], dev(dz=at))

    def half_along_z(src, at, part):
        s = z_slot(src, at)
        put(kv.at[z_slot(src), part], kv.at[s, part], rs.at[s, part], dev(dz=at))

    def from_z(src):
        s = z_slot(src)
        got(kv.at[s], rs.at[s, 0])

    for d in (1, -1, 2, -2):
        along_z(0, d)
    to_sides(0, 0)
    to_core(0, 0, 0)

    def turn(t, carry):
        rows = qkv[t].astype(jnp.float32)
        cosine, sine = cq[pl.ds(t, 1), :], sq[pl.ds(t, 1), :]
        head = rows[:9].reshape(72, HEAD)
        xs[pl.ds(pl.multiple_of(t * 80, 8), 72), :] = head * cosine + pltpu.roll(head, HEAD // 2, 1) * sine
        xs[pl.ds(pl.multiple_of(t * 80 + 72, 8), 8), :] = rows[9]
        return carry

    loading.wait()
    lax.fori_loop(0, LOCAL, turn, 0, unroll=4)
    for h in range(8):
        sks[h] = xs[pl.ds(64 + h, LOCAL, stride=80), :].astype(jnp.bfloat16)
        svs[h] = xs[pl.ds(72 + h, LOCAL, stride=80), :].astype(jnp.bfloat16)
    for d in range(4):
        pair = pl.ds(2 * ((y + d) % NY), 2)
        back = (4 - d) % 4
        if d == 0:
            keep(sks.at[pair], sk.at[0, y])
            keep(svs.at[pair], sv.at[0, y])
        else:
            put(sks.at[pair], sk.at[0, y], rsk.at[0, back], dev(dy=d))
            put(svs.at[pair], sv.at[0, y], rsv.at[0, back], dev(dy=d))

    def gather(t, carry):
        for h in range(8):
            two = [xs[pl.ds(t * 160 + 80 * j + h, 8, stride=8), :] for j in range(2)]
            qs[h, pl.ds(pl.multiple_of(t * 16, 16), 16), :] = jnp.concatenate(two, axis=0).astype(jnp.bfloat16)
        return carry

    lax.fori_loop(0, LOCAL // 2, gather, 0, unroll=2)
    for hr in range(2):
        for d in (0, 3, 1, 2):
            src = qs.at[2 * ((y + d) % NY) + (zh + hr) % 2]
            back = (4 - d) % 4
            if d == 0:
                keep(src, qb.at[hr, 0])
            else:
                put(src, qb.at[hr, back], rq.at[hr, back], dev(dy=d))

    def unit(u):
        k = min(u, 7 - u) if isinstance(u, int) else jnp.minimum(u, 7 - u)
        return u // 4, (k * (k + 1) // 2) % 4

    def token_block(hr, n, part):
        if n < 8:
            return kv[pl.ds(hr * 32 + 4 * n, 4), part].reshape(4 * BLOCK, HEAD)
        ref = sk if part == 0 else sv
        return ref[n - 8, :, (zh + hr) % 2].reshape(4 * LOCAL, HEAD)

    def query_tile(t):
        hr, d = unit(t // 2)
        floats = qb[hr, d, pl.ds(pl.multiple_of((t % 2) * ROWS, ROWS), ROWS), :].astype(jnp.float32) * SCALE
        high = floats.astype(jnp.bfloat16)
        low = (floats - high.astype(jnp.float32)).astype(jnp.bfloat16)
        return jnp.concatenate([high, low], axis=1)

    def score(t, n, buf, j):
        hr, d = unit(t // 2)
        keys = token_block(hr, n, 0)
        first, size = SPANS[n]
        keys = jnp.concatenate([keys, keys], axis=1)
        s = lax.dot_general(query_tile(t), keys, NT, preferred_element_type=jnp.float32)
        if n >= 8:
            token = (2 * ((y + d) % NY) + zh) * LOCAL + (t % 2) * (ROWS // GQ)
            row = token + lax.broadcasted_iota(jnp.int32, (ROWS, size), 0) // GQ
            col = lax.broadcasted_iota(jnp.int32, (ROWS, size), 1)
            col = (col // LOCAL) * (2 * LOCAL) + ((zh + n) % 2) * LOCAL + col % LOCAL
            s = jnp.where(col <= row, s, -1e30)
        buf[j, :, first:first + size] = s
        top = s[:, :128]
        for m in range(1, size // 128):
            top = jnp.maximum(top, s[:, m * 128:(m + 1) * 128])
        return top

    def weigh(t, n, buf, j, top):
        hr, _ = unit(t // 2)
        first, size = SPANS[n]
        weights = jnp.exp2(buf[j, :, first:first + size] - top).astype(jnp.bfloat16)
        values = token_block(hr, n, 1)
        values = jnp.concatenate([values, jnp.ones_like(values)], axis=1)
        return jnp.dot(weights, values, preferred_element_type=jnp.float32)

    def widest(top):
        return jnp.broadcast_to(jnp.max(top, axis=1, keepdims=True), (ROWS, 128))

    def stage(t, buf, j, tn=None, bufn=None):
        top, total = None, None
        peak = mx[t % 8][:, :1]
        for n in range(len(SPANS)):
            if tn is not None:
                part = score(tn, n, bufn, j)
                top = part if top is None else jnp.maximum(top, part)
            part = weigh(t, n, buf, j, peak)
            total = part if total is None else total + part
        if tn is not None:
            mx[tn % 8] = widest(top)
        hr, d = unit(t // 2)
        result = (total[:, :HEAD] / total[:, HEAD:]).reshape(ROWS // GQ, GQ, HEAD)
        at = pl.ds(pl.multiple_of((t % 2) * (ROWS // GQ), ROWS // GQ), ROWS // GQ)
        ob[hr, d, at] = result.astype(jnp.bfloat16)

    def head_of(hr):
        return 2 * y + (zh + hr) % 2

    def result_copy(u):
        hr, d = unit(u)
        return pltpu.make_async_remote_copy(
            src_ref=ob.at[hr, d], dst_ref=out.at[:, head_of(hr)],
            send_sem=osend.at[u], recv_sem=ro.at[hr, (4 - d) % 4],
            device_id=dev(dy=d), device_id_type=pl.DeviceIdType.MESH)

    def own_copy(u):
        hr, d = unit(u)
        return pltpu.make_async_copy(ob.at[hr, d], out.at[:, head_of(hr)], osend.at[u])

    def deliver(t):
        @pl.when((t % 2 == 1) & (t != 1) & (t != 15))
        def _():
            result_copy(t // 2).start()

        @pl.when((t == 1) | (t == 15))
        def _():
            own_copy(t // 2).start()

    def early(n, first=False):
        for j in range(4):
            for half, buf in ((0, g0), (1, g1)):
                t = 4 * half + j
                part = score(t, n, buf, j)
                mx[t] = part if first else jnp.maximum(mx[t], part)

    def later(n, first=False):
        for j in range(4):
            part = score(8 + j, n, g0, j)
            mx[j] = part if first else jnp.maximum(mx[j], part)

    first = (zl == 0).astype(jnp.int32)
    last = (zl == NH - 1).astype(jnp.int32)
    ka = 1 + 2 * last
    kb = 3 - first - last
    near = (0, ka, kb, 6 - ka - kb)
    def spread(half, k):
        to_sides(half, k)
        to_core(half, 0, k)

    from_z(-1)
    from_z(1)
    spread(0, near[1])
    for sign in (-1, 1):
        from_z(2 * sign)
        along_z(2 * sign, -sign)
    spread(0, near[2])
    relay(0, near[0])
    for sign in (-1, 1):
        from_z(3 * sign)
        half_along_z(3 * sign, -sign, (1 + sign) // 2)
    spread(0, near[3])
    for copy in kept[:2]:
        copy.wait()
    for d in (1, 2, 3):
        src = (y + d) % NY
        got(sk.at[0, src], rsk.at[0, d])
        got(sv.at[0, src], rsv.at[0, d])
    put(sk.at[0], rk, rsk.at[1, 0], dev(dz=2))
    put(sv.at[0], rv, rsv.at[1, 0], dev(dz=-2))
    relay(0, near[1])
    for n in (1, 2, 3):
        spread(1, n)
    relay(0, near[2])
    relay(0, near[3])
    for copy in kept[2:]:
        copy.wait()
    for d in (1, 3, 2):
        got(qb.at[0, d], rq.at[0, d])
    early(0, True)
    s = slot(1, 0, 0, 0)
    got(kv.at[s, 0], rs.at[s, 0])
    got(kv.at[s, 1], rs.at[s, 1])
    spread(1, 0)
    for n in range(4):
        full(0, 0, 1, n)
    early(1)
    for n in range(4):
        close(0, near[n])
    early(2)
    early(4)
    got(rk, rsk.at[1, 0])
    put(rk, sk.at[1], rsk.at[1, 1], dev(dz=2))
    got(rv, rsv.at[1, 0])
    put(rv, sv.at[1], rsv.at[1, 1], dev(dz=-2))
    for n in range(4):
        full(0, 1, 1, n)
        full(0, 2, 1, n)
    early(3)
    early(5)
    early(6)
    for n in (1, 2, 3):
        relay(1, n)
    for n in range(4):
        full(0, 3, 1, n)
    early(7)
    relay(1, 0)
    got(sk.at[1], rsk.at[1, 1])
    got(sv.at[1], rsv.at[1, 1])
    early(8)
    early(9)
    for t in range(8):
        mx[t] = widest(mx[t])

    def loop(start, step):
        def body(j, carry):
            step(j)
            deliver(start + j)
            return carry
        lax.fori_loop(0, 4, body, 0)

    def opening(j):
        stage(j, g0, j)

        @pl.when(j == 1)
        def _():
            for n in (1, 2, 3):
                close(1, n)

        @pl.when(j == 3)
        def _():
            close(1, 0)

    loop(0, opening)
    for d in (1, 3, 2):
        got(qb.at[1, d], rq.at[1, d])
    later(0, True)
    later(8)
    later(9)
    for n in range(4):
        full(1, 0, 1, n)
    later(1)
    later(2)
    later(4)
    loop(4, lambda j: stage(4 + j, g1, j))
    for n in range(4):
        full(1, 1, 1, n)
        full(1, 2, 1, n)
    later(3)
    later(5)
    later(6)
    for n in range(4):
        full(1, 3, 1, n)
    later(7)
    for j in range(4):
        mx[j] = widest(mx[j])
    loop(8, lambda j: stage(8 + j, g0, j, 12 + j, g1))
    loop(12, lambda j: stage(12 + j, g1, j))

    for wait in ends:
        wait()
    for u in range(8):
        if u in (0, 7):
            own_copy(u).wait()
        else:
            result_copy(u).wait_send()
    for hr in range(2):
        for d in (1, 2, 3):
            got(out.at[:, 2 * ((y + d) % NY) + (zh + hr) % 2], ro.at[hr, d])


def shards(qkv, key_codes, codebooks, value_codes, value_scales, block_ids):
    bf, f32 = jnp.bfloat16, jnp.float32
    dma = pltpu.SemaphoreType.DMA
    vmem = pl.BlockSpec(memory_space=pltpu.VMEM)
    return pl.pallas_call(
        kernel,
        out_shape=jax.ShapeDtypeStruct((LOCAL, 8, GQ, HEAD), bf),
        in_specs=[pl.BlockSpec(memory_space=pl.ANY)] + [vmem] * 4 + [pl.BlockSpec(memory_space=pltpu.SMEM), vmem],
        out_specs=pl.BlockSpec(memory_space=pl.ANY),
        scratch_shapes=[
            pltpu.VMEM((LOCAL, GQ + 2, 8, HEAD), bf),
            pltpu.VMEM((64, 2, BLOCK, HEAD), bf),
            pltpu.VMEM((8, LOCAL * GQ, HEAD), bf),
            pltpu.VMEM((8, LOCAL, HEAD), bf),
            pltpu.VMEM((8, LOCAL, HEAD), bf),
            pltpu.VMEM((2, 4, LOCAL * GQ, HEAD), bf),
            pltpu.VMEM((2, 4, 2, LOCAL, HEAD), bf),
            pltpu.VMEM((2, 4, 2, LOCAL, HEAD), bf),
            pltpu.VMEM((4, 2, LOCAL, HEAD), bf),
            pltpu.VMEM((4, 2, LOCAL, HEAD), bf),
            pltpu.VMEM((2, 4, LOCAL, GQ, HEAD), bf),
            pltpu.VMEM((LOCAL * 80, HEAD), f32),
            pltpu.VMEM((LOCAL, HEAD), f32),
            pltpu.VMEM((LOCAL, HEAD), f32),
            pltpu.VMEM((4, ROWS, WIDTH), f32),
            pltpu.VMEM((4, ROWS, WIDTH), f32),
            pltpu.VMEM((8, ROWS, 128), f32),
            dma((128,)), dma((64, 2)), dma((2, 4)), dma((2, 4)), dma((2, 4)),
            dma((2, 4)), dma((8,)), dma((8,)), dma,
        ],
        compiler_params=pltpu.CompilerParams(
            collective_id=0, has_side_effects=True, vmem_limit_bytes=60 * 2**20),
    )(qkv.transpose(0, 2, 1, 3), key_codes[:, 0].T, codebooks[0], value_codes[:, 0],
      value_scales.T, block_ids, rope_tables())


def solution(mesh):
    return jax.shard_map(
        shards,
        mesh=mesh,
        in_specs=(
            P(("outer", "inner"), None, None, None),
            P("outer", "inner", None),
            P("inner", None, None),
            P("outer", "inner", None),
            P("outer", "inner"),
            P("outer"),
        ),
        out_specs=P(("outer", "inner"), None, None, None),
        check_vma=False,
    )
```

```python
import functools
import math

import jax
import jax.numpy as jnp
import numpy as np
from jax import lax
from jax.experimental import pallas as pl
from jax.experimental.pallas import tpu as pltpu
from jax.sharding import PartitionSpec as P

rope_base = 500000.0
NX, NY, NZ, NH = 4, 4, 8, 4
BLOCK, HEAD, GQ, LOCAL, CODES, GROUPS, PREFIX = 128, 128, 8, 64, 256, 16, 4096
ROWS = 256
SCALE = 128**-0.5 * math.log2(math.e)
NT = (((1,), (1,)), ((), ()))
SPANS = [(512 * n, 512) for n in range(8)] + [(4096, 256), (4352, 256)]
WIDTH = 4608
DIRECT = (1, 0)


def rope_tables():
    step = np.float32(-2.0 * math.log(rope_base) / HEAD)
    inverse = np.exp((np.arange(64, dtype=np.float32) * step).astype(np.float64)).astype(np.float32).astype(np.float64)
    inverse = np.concatenate([inverse, inverse])
    fine = np.arange(BLOCK)[:, None] * inverse
    starts = np.concatenate([np.arange(32) * BLOCK, PREFIX + np.arange(8) * LOCAL])
    coarse = starts[:, None] * inverse
    table = np.concatenate([np.cos(fine), np.sin(fine), np.cos(coarse), np.sin(coarse)])
    return jnp.asarray(table.astype(np.float32))


def kernel(raw, codes, books, vcodes, scales, block, table, out,
           qkv, kv, qs, sks, svs, qb, sk, sv, rk, rv, ob, xs, cq, sq, g0, g1, mx,
           send, rs, rq, rsk, rsv, ro, loc, osend, load):
    o = lax.axis_index("outer")
    i = lax.axis_index("inner")
    zl, x, c = o // 8, (o // 2) % NX, o % 2
    y, zh = i // 2, i % 2
    z = zh * NH + zl

    def dev(dx=0, dy=0, dz=0, dc=0):
        z1 = (z + dz) % NZ
        outer = (z1 % NH) * 8 + ((x + dx) % NX) * 2 + (c + dc) % 2
        return {"outer": outer, "inner": ((y + dy) % NY) * 2 + z1 // NH}

    peers = [dev(dz=d) for d in (1, -1, 2, -2)] + [dev(dx=d) for d in (1, 2, 3)] + [dev(dc=1)]
    peers += [dev(dy=d) for d in (1, 2, 3)]
    barrier = pltpu.get_barrier_semaphore()
    for peer in peers:
        pl.semaphore_signal(barrier, inc=1, device_id=peer, device_id_type=pl.DeviceIdType.MESH)

    loading = pltpu.make_async_copy(raw, qkv, load)
    loading.start()

    def slot(half, side, core, k):
        return ((half * 4 + side) * 2 + core) * 4 + k

    def z_slot(src, at=0):
        half = (((z + src) % NZ) // NH + ((z + at) % NZ) // NH) % 2
        return slot(half, 0, 0, (src - at) % 4)

    def angles(start, rows):
        fine_c, fine_s = table[:rows], table[BLOCK:BLOCK + rows]
        base_c = table[pl.ds(2 * BLOCK + start, 1), :]
        base_s = table[pl.ds(2 * BLOCK + 40 + start, 1), :]
        lane = lax.broadcasted_iota(jnp.int32, (rows, HEAD), 1)
        sine = base_s * fine_c + base_c * fine_s
        return base_c * fine_c - base_s * fine_s, jnp.where(lane < HEAD // 2, -sine, sine)

    book_t = books[...].astype(jnp.float32).T
    entry = lax.broadcasted_iota(jnp.int32, (CODES, BLOCK), 0)
    parts = []
    for g in range(GROUPS):
        hot = jnp.where(entry == codes[g:g + 1, :], 1.0, 0.0).astype(jnp.bfloat16)
        rows = book_t[8 * g:8 * g + 8, :].astype(jnp.bfloat16)
        parts.append(jnp.dot(rows, hot, preferred_element_type=jnp.float32))
    keys = jnp.concatenate(parts, axis=0).T
    cosine, sine = angles(block[0], BLOCK)
    own = slot(0, 0, 0, 0)
    kv[own, 0] = (keys * cosine + pltpu.roll(keys, HEAD // 2, 1) * sine).astype(jnp.bfloat16)
    scale = jnp.broadcast_to(scales[...], (BLOCK, BLOCK)).T
    kv[own, 1] = (vcodes[...].astype(jnp.float32) * scale).astype(jnp.bfloat16)
    cq[...], sq[...] = angles(32 + i, LOCAL)

    pl.semaphore_wait(barrier, len(peers))

    sent, ends = [], []
    likes = {r.shape: r for r in (kv.at[0], kv.at[0, 0], sks.at[pl.ds(0, 2)], qb.at[0, 0], rk)}

    def put(src, dst, recv_sem, to):
        index = len(sent)
        sent.append(index)
        pltpu.make_async_remote_copy(
            src_ref=src, dst_ref=dst, send_sem=send.at[index], recv_sem=recv_sem,
            device_id=to, device_id_type=pl.DeviceIdType.MESH).start()
        like = likes[src.shape]
        ends.append(lambda: pltpu.make_async_copy(like, like, send.at[index]).wait())

    def got(dst, recv_sem):
        pltpu.make_async_copy(dst, dst, recv_sem).wait()

    kept = []

    def keep(src, dst):
        copy = pltpu.make_async_copy(src, dst, loc.at[len(kept)])
        copy.start()
        kept.append(copy)

    def full(half, side, core, k):
        s = slot(half, side, core, k)
        got(kv.at[s], rs.at[s, 0])

    def to_sides(half, k):
        src = kv.at[slot(half, 0, 0, k)]
        for side, dx in ((1, 1), (2, 3), (3, 2))[:2 + DIRECT[half]]:
            s = slot(half, side, 0, k)
            put(src, kv.at[s], rs.at[s, 0], dev(dx=dx))

    def to_core(half, side, k):
        s = slot(half, side, 1, k)
        put(kv.at[slot(half, side, 0, k)], kv.at[s], rs.at[s, 0], dev(dc=1))

    def relay(half, k):
        for side, dx in ((1, 1), (2, 3)):
            full(half, side, 0, k)
            s = slot(half, 3, 0, k)
            part = side - 1
            if not DIRECT[half]:
                put(kv.at[slot(half, side, 0, k), part], kv.at[s, part], rs.at[s, part], dev(dx=dx))
            to_core(half, side, k)

    def close(half, k):
        s = slot(half, 3, 0, k)
        if DIRECT[half]:
            got(kv.at[s], rs.at[s, 0])
        else:
            got(kv.at[s, 0], rs.at[s, 0])
            got(kv.at[s, 1], rs.at[s, 1])
        to_core(half, 3, k)

    def along_z(src, at):
        s = z_slot(src, at)
        put(kv.at[z_slot(src)], kv.at[s], rs.at[s, 0], dev(dz=at))

    def half_along_z(src, at, part):
        s = z_slot(src, at)
        put(kv.at[z_slot(src), part], kv.at[s, part], rs.at[s, part], dev(dz=at))

    def from_z(src):
        s = z_slot(src)
        got(kv.at[s], rs.at[s, 0])

    for d in (1, -1, 2, -2):
        along_z(0, d)
    to_sides(0, 0)
    to_core(0, 0, 0)

    def turn(t, carry):
        rows = qkv[t].astype(jnp.float32)
        cosine, sine = cq[pl.ds(t, 1), :], sq[pl.ds(t, 1), :]
        head = rows[:9].reshape(72, HEAD)
        xs[pl.ds(pl.multiple_of(t * 80, 8), 72), :] = head * cosine + pltpu.roll(head, HEAD // 2, 1) * sine
        xs[pl.ds(pl.multiple_of(t * 80 + 72, 8), 8), :] = rows[9]
        return carry

    loading.wait()
    lax.fori_loop(0, LOCAL, turn, 0, unroll=4)
    for h in range(8):
        sks[h] = xs[pl.ds(64 + h, LOCAL, stride=80), :].astype(jnp.bfloat16)
        svs[h] = xs[pl.ds(72 + h, LOCAL, stride=80), :].astype(jnp.bfloat16)
    for d in range(4):
        pair = pl.ds(2 * ((y + d) % NY), 2)
        back = (4 - d) % 4
        if d == 0:
            keep(sks.at[pair], sk.at[0, y])
            keep(svs.at[pair], sv.at[0, y])
        else:
            put(sks.at[pair], sk.at[0, y], rsk.at[0, back], dev(dy=d))
            put(svs.at[pair], sv.at[0, y], rsv.at[0, back], dev(dy=d))

    def gather(t, carry):
        for h in range(8):
            two = [xs[pl.ds(t * 160 + 80 * j + h, 8, stride=8), :] for j in range(2)]
            qs[h, pl.ds(pl.multiple_of(t * 16, 16), 16), :] = jnp.concatenate(two, axis=0).astype(jnp.bfloat16)
        return carry

    lax.fori_loop(0, LOCAL // 2, gather, 0, unroll=2)
    for hr in range(2):
        for d in (0, 3, 1, 2):
            src = qs.at[2 * ((y + d) % NY) + (zh + hr) % 2]
            back = (4 - d) % 4
            if d == 0:
                keep(src, qb.at[hr, 0])
            else:
                put(src, qb.at[hr, back], rq.at[hr, back], dev(dy=d))

    def unit(u):
        k = min(u, 7 - u) if isinstance(u, int) else jnp.minimum(u, 7 - u)
        return u // 4, (k * (k + 1) // 2) % 4

    def token_block(hr, n, part):
        if n < 8:
            return kv[pl.ds(hr * 32 + 4 * n, 4), part].reshape(4 * BLOCK, HEAD)
        ref = sk if part == 0 else sv
        return ref[n - 8, :, (zh + hr) % 2].reshape(4 * LOCAL, HEAD)

    def query_tile(t):
        hr, d = unit(t // 2)
        floats = qb[hr, d, pl.ds(pl.multiple_of((t % 2) * ROWS, ROWS), ROWS), :].astype(jnp.float32) * SCALE
        high = floats.astype(jnp.bfloat16)
        low = (floats - high.astype(jnp.float32)).astype(jnp.bfloat16)
        return jnp.concatenate([high, low], axis=1)

    def score(t, n, buf, j):
        hr, d = unit(t // 2)
        keys = token_block(hr, n, 0)
        first, size = SPANS[n]
        keys = jnp.concatenate([keys, keys], axis=1)
        s = lax.dot_general(query_tile(t), keys, NT, preferred_element_type=jnp.float32)
        if n >= 8:
            token = (2 * ((y + d) % NY) + zh) * LOCAL + (t % 2) * (ROWS // GQ)
            row = token + lax.broadcasted_iota(jnp.int32, (ROWS, size), 0) // GQ
            col = lax.broadcasted_iota(jnp.int32, (ROWS, size), 1)
            col = (col // LOCAL) * (2 * LOCAL) + ((zh + n) % 2) * LOCAL + col % LOCAL
            s = jnp.where(col <= row, s, -1e30)
        buf[j, :, first:first + size] = s
        top = s[:, :128]
        for m in range(1, size // 128):
            top = jnp.maximum(top, s[:, m * 128:(m + 1) * 128])
        return top

    def weigh(t, n, buf, j, top):
        hr, _ = unit(t // 2)
        first, size = SPANS[n]
        weights = jnp.exp2(buf[j, :, first:first + size] - top).astype(jnp.bfloat16)
        values = token_block(hr, n, 1)
        values = jnp.concatenate([values, jnp.ones_like(values)], axis=1)
        return jnp.dot(weights, values, preferred_element_type=jnp.float32)

    def widest(top):
        return jnp.broadcast_to(jnp.max(top, axis=1, keepdims=True), (ROWS, 128))

    def stage(t, buf, j, tn=None, bufn=None):
        top, total = None, None
        peak = mx[t % 8][:, :1]
        for n in range(len(SPANS)):
            if tn is not None:
                part = score(tn, n, bufn, j)
                top = part if top is None else jnp.maximum(top, part)
            part = weigh(t, n, buf, j, peak)
            total = part if total is None else total + part
        if tn is not None:
            mx[tn % 8] = widest(top)
        hr, d = unit(t // 2)
        result = (total[:, :HEAD] / total[:, HEAD:]).reshape(ROWS // GQ, GQ, HEAD)
        at = pl.ds(pl.multiple_of((t % 2) * (ROWS // GQ), ROWS // GQ), ROWS // GQ)
        ob[hr, d, at] = result.astype(jnp.bfloat16)

    def head_of(hr):
        return 2 * y + (zh + hr) % 2

    def result_copy(u):
        hr, d = unit(u)
        return pltpu.make_async_remote_copy(
            src_ref=ob.at[hr, d], dst_ref=out.at[:, head_of(hr)],
            send_sem=osend.at[u], recv_sem=ro.at[hr, (4 - d) % 4],
            device_id=dev(dy=d), device_id_type=pl.DeviceIdType.MESH)

    def own_copy(u):
        hr, d = unit(u)
        return pltpu.make_async_copy(ob.at[hr, d], out.at[:, head_of(hr)], osend.at[u])

    def deliver(t):
        @pl.when((t % 2 == 1) & (t != 1) & (t != 15))
        def _():
            result_copy(t // 2).start()

        @pl.when((t == 1) | (t == 15))
        def _():
            own_copy(t // 2).start()

    def early(n, first=False):
        for j in range(4):
            for half, buf in ((0, g0), (1, g1)):
                t = 4 * half + j
                part = score(t, n, buf, j)
                mx[t] = part if first else jnp.maximum(mx[t], part)

    def later(n, first=False):
        for j in range(4):
            part = score(8 + j, n, g0, j)
            mx[j] = part if first else jnp.maximum(mx[j], part)

    first = (zl == 0).astype(jnp.int32)
    last = (zl == NH - 1).astype(jnp.int32)
    ka = 1 + 2 * last
    kb = 3 - first - last
    near = (0, ka, kb, 6 - ka - kb)
    def spread(half, k):
        to_sides(half, k)
        to_core(half, 0, k)

    from_z(-1)
    from_z(1)
    spread(0, near[1])
    for sign in (-1, 1):
        from_z(2 * sign)
        along_z(2 * sign, -sign)
    spread(0, near[2])
    relay(0, near[0])
    for sign in (-1, 1):
        from_z(3 * sign)
        half_along_z(3 * sign, -sign, (1 + sign) // 2)
    spread(0, near[3])
    for n in (1, 2, 3):
        spread(1, n)
    for copy in kept[:2]:
        copy.wait()
    for d in (1, 2, 3):
        src = (y + d) % NY
        got(sk.at[0, src], rsk.at[0, d])
        got(sv.at[0, src], rsv.at[0, d])
    put(sk.at[0], rk, rsk.at[1, 0], dev(dz=2))
    put(sv.at[0], rv, rsv.at[1, 0], dev(dz=-2))
    relay(0, near[1])
    relay(0, near[2])
    relay(0, near[3])
    for copy in kept[2:]:
        copy.wait()
    for d in (1, 3, 2):
        got(qb.at[0, d], rq.at[0, d])
    early(0, True)
    s = slot(1, 0, 0, 0)
    got(kv.at[s, 0], rs.at[s, 0])
    got(kv.at[s, 1], rs.at[s, 1])
    spread(1, 0)
    for n in range(4):
        full(0, 0, 1, n)
    early(1)
    for n in range(4):
        close(0, near[n])
    early(2)
    early(4)
    got(rk, rsk.at[1, 0])
    put(rk, sk.at[1], rsk.at[1, 1], dev(dz=2))
    got(rv, rsv.at[1, 0])
    put(rv, sv.at[1], rsv.at[1, 1], dev(dz=-2))
    for n in range(4):
        full(0, 1, 1, n)
        full(0, 2, 1, n)
    early(3)
    for n in (1, 2, 3):
        relay(1, n)
    early(5)
    early(6)
    for n in range(4):
        full(0, 3, 1, n)
    early(7)
    relay(1, 0)
    got(sk.at[1], rsk.at[1, 1])
    got(sv.at[1], rsv.at[1, 1])
    early(8)
    early(9)
    for t in range(8):
        mx[t] = widest(mx[t])

    def loop(start, step):
        def body(j, carry):
            step(j)
            deliver(start + j)
            return carry
        lax.fori_loop(0, 4, body, 0)

    def opening(j):
        stage(j, g0, j)

        @pl.when(j == 1)
        def _():
            for n in (1, 2, 3):
                close(1, n)

        @pl.when(j == 3)
        def _():
            close(1, 0)

    loop(0, opening)
    for d in (1, 3, 2):
        got(qb.at[1, d], rq.at[1, d])
    later(0, True)
    later(8)
    later(9)
    for n in range(4):
        full(1, 0, 1, n)
    later(1)
    later(2)
    later(4)
    loop(4, lambda j: stage(4 + j, g1, j))
    for n in range(4):
        full(1, 1, 1, n)
        full(1, 2, 1, n)
    later(3)
    later(5)
    later(6)
    for n in range(4):
        full(1, 3, 1, n)
    later(7)
    for j in range(4):
        mx[j] = widest(mx[j])
    loop(8, lambda j: stage(8 + j, g0, j, 12 + j, g1))
    loop(12, lambda j: stage(12 + j, g1, j))

    for wait in ends:
        wait()
    for u in range(8):
        if u in (0, 7):
            own_copy(u).wait()
        else:
            result_copy(u).wait_send()
    for hr in range(2):
        for d in (1, 2, 3):
            got(out.at[:, 2 * ((y + d) % NY) + (zh + hr) % 2], ro.at[hr, d])


def shards(qkv, key_codes, codebooks, value_codes, value_scales, block_ids):
    bf, f32 = jnp.bfloat16, jnp.float32
    dma = pltpu.SemaphoreType.DMA
    vmem = pl.BlockSpec(memory_space=pltpu.VMEM)
    return pl.pallas_call(
        kernel,
        out_shape=jax.ShapeDtypeStruct((LOCAL, 8, GQ, HEAD), bf),
        in_specs=[pl.BlockSpec(memory_space=pl.ANY)] + [vmem] * 4 + [pl.BlockSpec(memory_space=pltpu.SMEM), vmem],
        out_specs=pl.BlockSpec(memory_space=pl.ANY),
        scratch_shapes=[
            pltpu.VMEM((LOCAL, GQ + 2, 8, HEAD), bf),
            pltpu.VMEM((64, 2, BLOCK, HEAD), bf),
            pltpu.VMEM((8, LOCAL * GQ, HEAD), bf),
            pltpu.VMEM((8, LOCAL, HEAD), bf),
            pltpu.VMEM((8, LOCAL, HEAD), bf),
            pltpu.VMEM((2, 4, LOCAL * GQ, HEAD), bf),
            pltpu.VMEM((2, 4, 2, LOCAL, HEAD), bf),
            pltpu.VMEM((2, 4, 2, LOCAL, HEAD), bf),
            pltpu.VMEM((4, 2, LOCAL, HEAD), bf),
            pltpu.VMEM((4, 2, LOCAL, HEAD), bf),
            pltpu.VMEM((2, 4, LOCAL, GQ, HEAD), bf),
            pltpu.VMEM((LOCAL * 80, HEAD), f32),
            pltpu.VMEM((LOCAL, HEAD), f32),
            pltpu.VMEM((LOCAL, HEAD), f32),
            pltpu.VMEM((4, ROWS, WIDTH), f32),
            pltpu.VMEM((4, ROWS, WIDTH), f32),
            pltpu.VMEM((8, ROWS, 128), f32),
            dma((128,)), dma((64, 2)), dma((2, 4)), dma((2, 4)), dma((2, 4)),
            dma((2, 4)), dma((8,)), dma((8,)), dma,
        ],
        compiler_params=pltpu.CompilerParams(
            collective_id=0, has_side_effects=True, vmem_limit_bytes=60 * 2**20),
    )(qkv.transpose(0, 2, 1, 3), key_codes[:, 0].T, codebooks[0], value_codes[:, 0],
      value_scales.T, block_ids, rope_tables())


def solution(mesh):
    return jax.shard_map(
        shards,
        mesh=mesh,
        in_specs=(
            P(("outer", "inner"), None, None, None),
            P("outer", "inner", None),
            P("inner", None, None),
            P("outer", "inner", None),
            P("outer", "inner"),
            P("outer"),
        ),
        out_specs=P(("outer", "inner"), None, None, None),
        check_vma=False,
    )
```
